32 devices in a mesh: gy: 8 (over y, x, core), gz: 4 (over z).
Axes of the slice: x: 2, y: 2, z: 4, core: 2. Of those that a mesh axis runs over, the one named last changes fastest.
Arguments:
- state: float32 [8, 5, 256, 512], P(None, None, 'gy', 'gz'), may hold values from -6 to 6
- conduct: float32 [8, 256, 512], P(None, 'gy', 'gz'), may hold values from 0.3 to 3
- y_bands: float32 [8, 5, 256, 512], P(None, None, 'gy', 'gz'), may hold values from -250 to 541, as said below
- z_bands: float32 [8, 5, 256, 512], P(None, None, 'gy', 'gz'), may hold values from -250 to 541, as said below
Outputs:
- new_state: float32 [8, 5, 256, 512], P(None, None, 'gy', 'gz')
The draws below stay inside these ranges and needn't reach their ends.
Inputs may be any that keep to these rules, and one draw needn't show every extreme that they name: `y_bands`: in every cell band 2 exceeds the sum of the magnitudes of bands 0, 1, 3 and 4 by 0.03 or more; bands 1 and 3 are negative, bands 0 and 4 are not positive. `z_bands`: in every cell band 2 exceeds the sum of the magnitudes of bands 0, 1, 3 and 4 by 0.03 or more; bands 1 and 3 are negative, bands 0 and 4 are not positive.
All inputs are finite; a program needn't handle non-finite values.
Results may differ from the reference program's by a relative error of at most 0.0003.
Values sent between devices are 32-bit elements; how exact they have to be, the bound alone decides.
A program may use at most 192 MiB of HBM per device.

```python
import math
import jax
import jax.numpy as jnp
from jax import lax

NV = 5
X = 8
NY = 256
NZ = 512


def band_table(key):
    subkeys = jax.random.split(key, 5)
    grid_shape = (X, NY, NZ)
    near_low = -jnp.exp(jax.random.uniform(subkeys[0], grid_shape, jnp.float32, math.log(60.0), math.log(240.0)))
    near_up = -jnp.exp(jax.random.uniform(subkeys[1], grid_shape, jnp.float32, math.log(60.0), math.log(240.0)))
    margin = jnp.exp(jax.random.uniform(subkeys[2], grid_shape, jnp.float32, math.log(0.04), math.log(0.12)))
    far_low = -jax.random.uniform(subkeys[3], grid_shape, jnp.float32, 0.0, 20.0)
    far_up = -jax.random.uniform(subkeys[4], grid_shape, jnp.float32, 0.0, 20.0)
    middle = margin + jnp.abs(far_low) + jnp.abs(near_low) + jnp.abs(near_up) + jnp.abs(far_up)
    return jnp.stack([far_low, near_low, middle, near_up, far_up], axis=1)


def draw_y_bands(key, part):
    return band_table(jax.random.fold_in(key, 11))


def draw_z_bands(key, part):
    return band_table(jax.random.fold_in(key, 23))


def shard_levels(rng, dims, cuts, low, largest):
    def one(position, blocks):
        draws = jax.random.uniform(jax.random.fold_in(jax.random.fold_in(rng, 6), position), (blocks,), jnp.float32, low / len(cuts), largest / len(cuts))
        return jnp.repeat(jnp.exp(draws), dims[position] // blocks).reshape((-1,) + (1,) * (len(dims) - position - 1))

    factor_of = one(*cuts[0])
    for cut in cuts[1:]:
        factor_of = factor_of * one(*cut)
    return factor_of


def scatter_about(rng, extent, deviation, reach, shards=(), held_as=jnp.bfloat16):
    values = deviation * jax.random.normal(rng, extent, jnp.float32)
    if shards:
        values = values * shard_levels(rng, extent, shards, -0.22, 0.18)
    return jnp.clip(values, -reach, reach).astype(held_as)


def setup_inputs(seed: int = 0) -> dict:
    keys = jax.random.split(jax.random.key(seed), 5)
    state = scatter_about(keys[0], (X, NV, NY, NZ), 1.0, 6.0, ((2, 8), (3, 4)), jnp.float32)
    conduct = jnp.clip(jnp.exp(math.log(3.0) - 2.3025851 * jax.random.uniform(keys[1], (X, NY, NZ), jnp.float32) ** shard_levels(keys[1], (X, NY, NZ), ((1, 8), (2, 4)), -0.2, 0.2)), 0.3, 3.0)
    y_bands = draw_y_bands(jax.random.fold_in(keys[4], 71), 0)
    z_bands = draw_z_bands(jax.random.fold_in(keys[4], 71), 0)
    return dict(state=state, conduct=conduct, y_bands=y_bands, z_bands=z_bands)


flux_rate = 0.2


def penta_lines(bands, rhs):
    count = rhs.shape[0]
    places = jnp.arange(count)[:, None, None]
    far_low = jnp.where(places >= 2, bands[0], jnp.float32(0.0))
    near_low = jnp.where(places >= 1, bands[1], jnp.float32(0.0))
    middle = bands[2]
    near_up = jnp.where(places <= count - 2, bands[3], jnp.float32(0.0))
    far_up = jnp.where(places <= count - 3, bands[4], jnp.float32(0.0))
    coef_zero = jnp.zeros(middle.shape[1:], jnp.float32)
    value_zero = jnp.zeros(rhs.shape[1:], jnp.float32)

    def forward(carry, pieces):
        last_p, last_q, last_y, older_p, older_q, older_y = carry
        coef_a, coef_b, coef_c, coef_d, coef_e, value = pieces
        reduced = coef_b - coef_a * older_p
        pivot = coef_c - coef_a * older_q - reduced * last_p
        new_p = (coef_d - reduced * last_q) / pivot
        new_q = coef_e / pivot
        new_y = (value - coef_a * older_y - reduced * last_y) / pivot
        return (new_p, new_q, new_y, last_p, last_q, last_y), (new_p, new_q, new_y)

    start = (coef_zero, coef_zero, value_zero, coef_zero, coef_zero, value_zero)
    unused, factors = lax.scan(forward, start, (far_low, near_low, middle, near_up, far_up, rhs))

    def backward(carry, pieces):
        later_one, later_two = carry
        gain_p, gain_q, scaled = pieces
        result = scaled - gain_p * later_one - gain_q * later_two
        return (result, later_one), result

    unused, solved = lax.scan(backward, (value_zero, value_zero), factors, reverse=True)
    return solved


def plane_step(pieces):
    field_now, kappa_now, y_coef, z_coef = pieces
    kappa = jnp.pad(kappa_now, 1)
    field = jnp.pad(field_now, ((0, 0), (1, 1), (1, 1)))
    centre = field[:, 1:-1, 1:-1]
    middle_k = kappa[1:-1, 1:-1]
    north = 0.5 * (middle_k + kappa[2:, 1:-1])
    south = 0.5 * (middle_k + kappa[:-2, 1:-1])
    upward = 0.5 * (middle_k + kappa[1:-1, 2:])
    downward = 0.5 * (middle_k + kappa[1:-1, :-2])
    flux = north * (field[:, 2:, 1:-1] - centre) - south * (centre - field[:, :-2, 1:-1]) + upward * (field[:, 1:-1, 2:] - centre) - downward * (centre - field[:, 1:-1, :-2])
    flux_rhs = centre + flux_rate * flux
    after_y = jnp.transpose(penta_lines(y_coef[:, :, None, :], jnp.transpose(flux_rhs, (1, 0, 2))), (1, 0, 2))
    z_solved = penta_lines(jnp.transpose(z_coef, (0, 2, 1))[:, :, None, :], jnp.transpose(after_y, (2, 0, 1)))
    return jnp.transpose(z_solved, (1, 2, 0))


def reference(state, conduct, y_bands, z_bands):
    return lax.map(plane_step, (state, conduct, y_bands, z_bands))
```

```python
import functools
import jax
import jax.numpy as jnp
from jax import lax
from jax.experimental import pallas as pl
from jax.experimental.pallas import tpu as pltpu
from jax.sharding import PartitionSpec as P

flux_tenth = 0.1
UNROLL = 32
MESH = pl.DeviceIdType.MESH
ROWS = 32
PACK = 20
STEP = ROWS + 1
HALF = ROWS // 2


def rows_loop(count, body, carry, unroll=UNROLL):
    if unroll >= count:
        for place in range(count):
            carry = body(place, carry)
        return carry

    def group(number, state):
        for inner in range(unroll):
            state = body(number * unroll + inner, state)
        return state

    return lax.fori_loop(0, count // unroll, group, carry)


def mm(a, b):
    return (
        a[0] * b[0] + a[1] * b[2],
        a[0] * b[1] + a[1] * b[3],
        a[2] * b[0] + a[3] * b[2],
        a[2] * b[1] + a[3] * b[3],
    )


def mv(a, x):
    return (a[0] * x[0] + a[1] * x[1], a[2] * x[0] + a[3] * x[1])


def plus(a, b):
    return tuple(x + y for x, y in zip(a, b))


def minus(a, b):
    return tuple(x - y for x, y in zip(a, b))


def negative(a):
    return tuple(-x for x in a)


def one_minus_inverse(k):
    m00, m01, m10, m11 = 1.0 - k[0], -k[1], -k[2], 1.0 - k[3]
    scale = 1.0 / (m00 * m11 - m01 * m10)
    return (m11 * scale, -m01 * scale, -m10 * scale, m00 * scale)


def factor_segment(band, coefs, spikes):
    zero = jnp.zeros((8, 128), jnp.float32)

    def one_row(j, carry, left):
        p1, q1, p2, q2, l01, l11, l02, l12 = carry
        a, b, c, d, e = (band(k, j) for k in range(5))
        red = b - a * p2
        inv = 1.0 / (c - a * q2 - red * p1)
        p = (d - red * q1) * inv
        q = e * inv
        ai = a * inv
        ri = red * inv
        if left == 0:
            l0, l1 = ai, b * inv
        elif left == 1:
            l0, l1 = -ri * l01, ai - ri * l11
        else:
            l0 = -ai * l02 - ri * l01
            l1 = -ai * l12 - ri * l11
        for number, item in enumerate((ai, ri, inv, p, q)):
            coefs[j, number] = item
        spikes[j, 0] = l0
        spikes[j, 1] = l1
        return (p, q, p1, q1, l0, l1, l01, l11)

    carry = (zero,) * 8
    carry = one_row(0, carry, 0)
    carry = one_row(1, carry, 1)
    carry = rows_loop(ROWS - 2, lambda j, c: one_row(j + 2, c, 2), carry, 30)

    def back(i, carry):
        j = ROWS - 1 - i
        one, two = carry
        p, q = coefs[j, 3], coefs[j, 4]
        start = (spikes[j, 0], spikes[j, 1], zero, zero)
        new = tuple(s - p * x - q * y for s, x, y in zip(start, one, two))
        for number in range(4):
            spikes[j, number] = new[number]
        return (new, one)

    minus_one = zero - 1.0
    rows_loop(ROWS, back, ((zero, zero, minus_one, zero), (zero, zero, zero, minus_one)))


def forward_values(rhs, coefs, values):
    zero = jnp.zeros((8, 128), jnp.float32)

    def row(j, carry):
        one, two = carry
        ai, ri, inv = (coefs[j, k] for k in range(3))
        new = tuple(f * inv - ai * y - ri * x for f, x, y in zip(rhs(j), one, two))
        for number in range(5):
            values[j, number] = new[number]
        return (new, one)

    rows_loop(ROWS, row, ((zero,) * 5, (zero,) * 5))


def backward_values(coefs, values):
    zero = jnp.zeros((8, 128), jnp.float32)

    def row(i, carry):
        j = ROWS - 1 - i
        one, two = carry
        p, q = coefs[j, 3], coefs[j, 4]
        new = tuple(values[j, v] - p * one[v] - q * two[v] for v in range(5))
        for number in range(5):
            values[j, number] = new[number]
        return (new, one)

    rows_loop(ROWS, row, ((zero,) * 5, (zero,) * 5))


def finish_values(values, spikes, tails, heads, put):
    def row(j, carry):
        l0, l1, r0, r1 = (spikes[j, k] for k in range(4))
        for v in range(5):
            put(
                j,
                v,
                values[j, v]
                - (l0 * tails[0][v] + l1 * tails[1][v])
                - (r0 * heads[0][v] + r1 * heads[1][v]),
            )
        return carry

    rows_loop(ROWS, row, 0)


def end_spikes(spikes):
    low, high = (0, 1), (ROWS - 2, ROWS - 1)
    take = lambda rows, first: tuple(spikes[r, first + c] for r in rows for c in range(2))
    return take(low, 0), take(high, 0), take(low, 2), take(high, 2)


def chain_factor(count, matrices):
    factors = []
    beta = None
    for i in range(count):
        lh, lt, rh, rt = matrices(i)
        if i == 0:
            factors.append((None, None, None, None, rh, rt))
            beta = rt
            continue
        m = one_minus_inverse(mm(lh, beta))
        delta = mm(m, rh)
        ltb = mm(lt, beta)
        beta = plus(rt, mm(ltb, delta))
        factors.append((lh, lt, m, ltb, delta, beta))
    return factors


def chain_values(count, factors, ends):
    gammas, alphas = [], []
    for i in range(count):
        gh, gt = ends(i)
        if i:
            lh, lt, m, ltb = factors[i][:4]
            alpha = alphas[-1]
            gh = mv(m, minus(gh, mv(lh, alpha)))
            gt = plus(minus(gt, mv(lt, alpha)), mv(ltb, gh))
        gammas.append(gh)
        alphas.append(gt)
    heads, tails = [None] * count, [None] * count
    heads[-1], tails[-1] = gammas[-1], alphas[-1]
    for i in range(count - 2, -1, -1):
        heads[i] = minus(gammas[i], mv(factors[i][4], heads[i + 1]))
        tails[i] = minus(alphas[i], mv(factors[i][5], heads[i + 1]))
    return heads, tails


def merge_matrices(left, right):
    lha, lta, rha, rta = left
    lhb, ltb, rhb, rtb = right
    n = one_minus_inverse(mm(rta, lhb))
    l_tau = mm(n, lta)
    r_tau = negative(mm(n, mm(rta, rhb)))
    l_eta = negative(mm(lhb, l_tau))
    r_eta = minus(rhb, mm(lhb, r_tau))
    lh = minus(lha, mm(rha, l_eta))
    rh = negative(mm(rha, r_eta))
    lt = negative(mm(ltb, l_tau))
    rt = minus(rtb, mm(ltb, r_tau))
    use = (n, rta, lhb, rha, ltb, l_tau, r_tau, l_eta, r_eta)
    return (lh, lt, rh, rt), use


def merge_values(use, gha, gta, ghb, gtb):
    n, rta, lhb, rha, ltb = use[:5]
    tau = mv(n, minus(gta, mv(rta, ghb)))
    eta = minus(ghb, mv(lhb, tau))
    return minus(gha, mv(rha, eta)), minus(gtb, mv(ltb, tau)), tau, eta


def split_values(use, tau, eta, tail, head):
    l_tau, r_tau, l_eta, r_eta = use[5:]
    inner_tail = minus(minus(tau, mv(l_tau, tail)), mv(r_tau, head))
    inner_head = minus(minus(eta, mv(l_eta, tail)), mv(r_eta, head))
    return inner_tail, inner_head


def up(items, amount):
    return tuple(pltpu.roll(x, 8 - amount, 0) for x in items)


def down(items, amount):
    return tuple(pltpu.roll(x, amount, 0) for x in items)


def flipped(index, mask):
    result, bit = index, 1
    while bit <= mask:
        if mask & bit:
            result = result + bit - 2 * bit * lax.rem(index // bit, 2)
        bit *= 2
    return result


def kernel(
    gy, gz, state_h, conduct_h, yb_h, zb_h, zval, zspike, ends_ref,
    yb, zb, field, zsend, zrecv,
    ycoef, yspike, yval, zcoef, zbt, yplane, plane,
    ym_out, ym_in, yv_out, yv_in, yr_out, yr_in, zm_all, zv_all, ht_all,
    in_sem, yh_s, yh_r, zh_s, zh_r, ym_s, ym_r, yv_s, yv_r, yr_s, yr_r,
    zm_s, zm_r, zv_s, zv_r, own_sem,
):
    me, mz = lax.axis_index("gy"), lax.axis_index("gz")
    step = gy // 8
    lanes = lax.broadcasted_iota(jnp.int32, (8, 128), 1)
    subs = lax.broadcasted_iota(jnp.int32, (8, 128), 0)
    seg = lax.rem(subs, 4)
    zero = jnp.zeros((8, 128), jnp.float32)

    inside = pl.ds(1, ROWS)
    loads = [
        [pltpu.make_async_copy(src.at[x], dst(x), in_sem.at[k, x]) for x in range(8)]
        for k, (src, dst) in enumerate(
            (
                (state_h, lambda x: field.at[pl.ds(0, 5), inside, x]),
                (conduct_h, lambda x: field.at[5, inside, x]),
                (yb_h, lambda x: yb.at[:, :, x]),
                (zb_h, lambda x: zb.at[:, :, x]),
            )
        )
    ]
    for load in loads:
        for copy in load:
            copy.start()

    def loaded(k):
        for copy in loads[k]:
            copy.wait()

    barrier = pltpu.get_barrier_semaphore()
    for k in range(1, gy):
        pl.semaphore_signal(
            barrier, inc=1, device_id=(lax.rem(me + k, gy), mz), device_id_type=MESH
        )
    for k in range(1, gz):
        pl.semaphore_signal(
            barrier, inc=1, device_id=(me, lax.rem(mz + k, gz)), device_id_type=MESH
        )

    loaded(0)
    loaded(1)

    def pack_row(j, carry):
        a0, a1, b0, b1 = carry
        for v in range(6):
            tile = field[v, j + 1]
            place = (v % 4) * ROWS + j
            moved = pltpu.roll(tile, (place + 1) % 128, 1)
            at_a = lanes == place
            at_b = lanes == (place + 1) % 128
            if v < 4:
                a0, b0 = jnp.where(at_a, moved, a0), jnp.where(at_b, moved, b0)
            else:
                a1, b1 = jnp.where(at_a, moved, a1), jnp.where(at_b, moved, b1)
        return (a0, a1, b0, b1)

    a0, a1, b0, b1 = rows_loop(ROWS, pack_row, (zero,) * 4)
    zsend[0, 0], zsend[0, 1], zsend[1, 0], zsend[1, 1] = a0, a1, b0, b1
    pl.semaphore_wait(barrier, gy + gz - 2)

    def remote(src, dst, send, recv, there):
        return pltpu.make_async_remote_copy(
            src_ref=src, dst_ref=dst, send_sem=send, recv_sem=recv,
            device_id=there, device_id_type=MESH,
        )

    prev_y, next_y = lax.rem(me + gy - 1, gy), lax.rem(me + 1, gy)
    prev_z, next_z = lax.rem(mz + gz - 1, gz), lax.rem(mz + 1, gz)
    z_fwd = remote(zsend.at[0], zrecv.at[0], zh_s.at[0], zh_r.at[0], (me, next_z))
    z_bwd = remote(zsend.at[1], zrecv.at[1], zh_s.at[1], zh_r.at[1], (me, prev_z))
    y_fwd = remote(field.at[:, ROWS], field.at[:, 0], yh_s.at[0], yh_r.at[0], (next_y, mz))
    y_bwd = remote(field.at[:, 1], field.at[:, ROWS + 1], yh_s.at[1], yh_r.at[1], (prev_y, mz))
    pl.when(mz < gz - 1)(z_fwd.start)
    pl.when(mz > 0)(z_bwd.start)
    pl.when(me < gy - 1)(y_fwd.start)
    pl.when(me > 0)(y_bwd.start)

    @pl.when(mz == 0)
    def _():
        zrecv[0] = jnp.zeros((2, 8, 128), jnp.float32)

    @pl.when(mz == gz - 1)
    def _():
        zrecv[1] = jnp.zeros((2, 8, 128), jnp.float32)

    @pl.when(me == 0)
    def _():
        field[:, 0] = jnp.zeros((6, 8, 128), jnp.float32)

    @pl.when(me == gy - 1)
    def _():
        field[:, ROWS + 1] = jnp.zeros((6, 8, 128), jnp.float32)

    loaded(2)
    factor_segment(
        lambda k, j: yb[k, j], ycoef, yspike
    )
    for number, item in enumerate(sum(end_spikes(yspike), ())):
        ym_out[number] = item

    place_of_mine = me // step
    owner = lax.rem(me, step) == 0

    def scatter(out, into, rows, send, recv, own, finish):
        for k in (6, 7, 4, 5, 2, 3, 1, 0):
            x = flipped(place_of_mine, k)
            source = out.at[:, x]
            target = into.at[me]
            away = remote(source, target, send.at[k], recv.at[me], (x * step, mz))
            here = pltpu.make_async_copy(source, target, own)
            act = (lambda c: c.wait_send()) if finish else (lambda c: c.start())
            if k:
                act(away)
            else:
                if step > 1:
                    pl.when(jnp.logical_not(owner))(lambda: act(away))
                local = here.wait if finish else here.start
                pl.when(owner)(local) if step > 1 else local()

    def scatter_arrived(out, into, rows, send, recv):
        for k in range(1, gy):
            i = lax.rem(me + k, gy)
            source = out.at[:, 0]
            target = into.at[i]
            remote(source, target, send.at[0], recv.at[i], (i, mz)).wait_recv()

    scatter(ym_out, ym_in, 16, ym_s, ym_r, own_sem.at[0], False)

    @pl.when(mz > 0)
    def _():
        z_fwd.wait_recv()

    @pl.when(mz < gz - 1)
    def _():
        z_bwd.wait_recv()

    @pl.when(me > 0)
    def _():
        y_fwd.wait_recv()

    @pl.when(me < gy - 1)
    def _():
        y_bwd.wait_recv()

    def shifted(j, v):
        tile = field[v, j + 1]
        place = (v % 4) * ROWS + j
        low = pltpu.roll(zrecv[0, v // 4], (128 - place) % 128, 1)
        high = pltpu.roll(zrecv[1, v // 4], (254 - place) % 128, 1)
        before = jnp.where(lanes == 0, low, pltpu.roll(tile, 1, 1))
        after = jnp.where(lanes == 127, high, pltpu.roll(tile, 127, 1))
        return tile, before, after

    def flux_rhs(j):
        k_here, k_before, k_after = shifted(j, 5)
        north = flux_tenth * (k_here + field[5, j + 2])
        south = flux_tenth * (k_here + field[5, j])
        upward = flux_tenth * (k_here + k_after)
        downward = flux_tenth * (k_here + k_before)
        result = []
        for v in range(5):
            here, before, after = shifted(j, v)
            result.append(
                here
                + (north * (field[v, j + 2] - here) - south * (here - field[v, j]))
                + (upward * (after - here) - downward * (here - before))
            )
        return result

    forward_values(flux_rhs, ycoef, yval)
    backward_values(ycoef, yval)
    for number, r in enumerate((0, 1, ROWS - 2, ROWS - 1)):
        for v in range(5):
            yv_out[5 * number + v] = yval[r, v]
    scatter(yv_out, yv_in, PACK, yv_s, yv_r, own_sem.at[1], False)

    loaded(3)

    def turn(source, target, k):
        for g in range(2):
            turned = source[k, pl.ds(g * HALF, HALF)].reshape(128, 128).T
            for part in range(4):
                rows = turned[part * ROWS : (part + 1) * ROWS]
                target[k, pl.ds((4 * g + part) * STEP, ROWS), :] = rows

    for k in range(5):
        turn(zb, zbt, k)
    scatter_done = functools.partial(scatter, finish=True)

    def owner_solve():
        scatter_arrived(ym_out, ym_in, 16, ym_s, ym_r)

        def matrices(i):
            rows = [
                jnp.broadcast_to(ym_in[i, pl.ds(q, 1), :], (8, 128)) for q in range(16)
            ]
            return tuple(tuple(rows[4 * b : 4 * b + 4]) for b in range(4))

        factors = chain_factor(gy, matrices)
        scatter_arrived(yv_out, yv_in, PACK, yv_s, yv_r)

        def ends(i):
            parts = [yv_in[i, pl.ds(5 * q, 5), :] for q in range(4)]
            parts = [jnp.concatenate([x, jnp.zeros((3, 128), jnp.float32)], axis=0) for x in parts]
            return (parts[0], parts[1]), (parts[2], parts[3])

        heads, tails = chain_values(gy, factors, ends)
        for i in range(gy):
            before = tails[i - 1] if i else (zero, zero)
            behind = heads[i + 1] if i < gy - 1 else (zero, zero)
            for q, item in enumerate(before + behind):
                yr_out[i, pl.ds(5 * q, 5), :] = item[0:5]

    def ret(k):
        i = flipped(me, k)
        source = yr_out.at[i]
        target = yr_in.at[:, place_of_mine]
        return source, target, i

    def owner_part():
        scatter_done(ym_out, ym_in, 16, ym_s, ym_r, own_sem.at[0]) if step == 1 else None
        scatter_done(yv_out, yv_in, PACK, yv_s, yv_r, own_sem.at[1]) if step == 1 else None
        owner_solve()
        for k in sorted(range(1, gy), key=lambda k: (6, 7, 4, 5, 2, 3, 1).index(k) if k < 8 else -k):
            source, target, i = ret(k)
            remote(source, target, yr_s.at[k], yr_r.at[place_of_mine], (i, mz)).start()
        source, target, i = ret(0)
        pltpu.make_async_copy(source, target, own_sem.at[2]).start()

    if step > 1:
        scatter_done(ym_out, ym_in, 16, ym_s, ym_r, own_sem.at[0])
        scatter_done(yv_out, yv_in, PACK, yv_s, yv_r, own_sem.at[1])
        pl.when(owner)(owner_part)
    else:
        owner_part()

    factor_segment(lambda k, j: zbt[k, pl.ds(j, 8, stride=STEP), :], zcoef, zspike)
    level_0 = end_spikes(zspike)
    level_1, use_1 = merge_matrices(level_0, tuple(up(m, 1) for m in level_0))
    level_2, use_2 = merge_matrices(level_1, tuple(up(m, 2) for m in level_1))

    def pack_four(tiles):
        packed = tiles[0]
        for k in range(1, 4):
            packed = jnp.where(seg == k, pltpu.roll(tiles[k], k, 0), packed)
        return packed

    def partners(act):
        for away in range(gz - 1, 0, -1):
            pl.when(mz + away < gz)(functools.partial(act, mz + away))
            pl.when(mz - away >= 0)(functools.partial(act, mz - away))

    def gather(ref, send, recv):
        def act(there):
            remote(ref.at[mz], ref.at[mz], send.at[there], recv.at[mz], (me, there)).start()

        partners(act)

    def gathered(ref, send, recv):
        def act(there):
            remote(ref.at[mz], ref.at[there], send.at[there], recv.at[there], (me, there)).wait_recv()

        partners(act)

    def gather_sent(ref, send, recv):
        def act(there):
            remote(ref.at[mz], ref.at[mz], send.at[there], recv.at[mz], (me, there)).wait_send()

        partners(act)

    for b in range(4):
        zm_all[mz, b] = pack_four(level_2[b])
    gather(zm_all, zm_s, zm_r)

    def y_returned():
        for k in range(8):
            x = flipped(place_of_mine, k)
            target = yr_in.at[:, x]
            away = remote(yr_out.at[0], target, yr_s.at[0], yr_r.at[x], (x * step, mz))
            here = pltpu.make_async_copy(yr_out.at[0], target, own_sem.at[2])
            if k:
                away.wait_recv()
            elif step > 1:
                pl.when(jnp.logical_not(owner))(away.wait_recv)
                pl.when(owner)(here.wait)
            else:
                here.wait()

    y_returned()
    got = [[yr_in[5 * q + v] for v in range(5)] for q in range(4)]

    def put_y(j, v, tile):
        yplane[v, j] = tile

    finish_values(yval, yspike, got[:2], got[2:], put_y)
    for v in range(5):
        turn(yplane, plane, v)

    forward_values(
        lambda j: [plane[v, pl.ds(j, 8, stride=STEP), :] for v in range(5)], zcoef, zval
    )
    backward_values(zcoef, zval)
    merged = []
    for v in range(5):
        gh = (zval[0, v], zval[1, v])
        gt = (zval[ROWS - 2, v], zval[ROWS - 1, v])
        gh1, gt1, tau1, eta1 = merge_values(use_1, gh, gt, up(gh, 1), up(gt, 1))
        gh2, gt2, tau2, eta2 = merge_values(use_2, gh1, gt1, up(gh1, 2), up(gt1, 2))
        merged.append((gh2 + gt2, tau1, eta1, tau2, eta2))
    for q in range(4):
        zv_all[mz, q] = pack_four([merged[v][0][q] for v in range(4)])
    zv_all[mz, 4] = pack_four([merged[4][0][q] for q in range(4)])
    gather(zv_all, zv_s, zv_r)

    gathered(zm_all, zm_s, zm_r)

    def spread(tile, k):
        result = tile
        for r in range(4):
            if r != k:
                result = jnp.where(seg == r, pltpu.roll(tile, (r - k) % 8, 0), result)
        return result

    def z_matrices(i):
        return tuple(tuple(spread(zm_all[i, b], k) for k in range(4)) for b in range(4))

    factors = chain_factor(gz, z_matrices)
    gathered(zv_all, zv_s, zv_r)

    def z_ends(i):
        return (zv_all[i, 0], zv_all[i, 1]), (zv_all[i, 2], zv_all[i, 3])

    def z_ends_last(i):
        tiles = [pltpu.roll(zv_all[i, 4], (8 - q) % 8, 0) if q else zv_all[i, 4] for q in range(4)]
        return (tiles[0], tiles[1]), (tiles[2], tiles[3])

    for number, ends in enumerate((z_ends, z_ends_last)):
        heads, tails = chain_values(gz, factors, ends)
        for i in range(gz):
            before = tails[i - 1] if i else (zero, zero)
            behind = heads[i + 1] if i < gz - 1 else (zero, zero)
            for q, item in enumerate(before + behind):
                ht_all[i, 4 * number + q] = item
    tails_in, heads_in = [[], []], [[], []]
    for v in range(5):
        base, shift = (0, v) if v < 4 else (4, 0)
        outer = tuple(ht_all[mz, base + q] for q in range(4))
        outer = up(outer, shift) if shift else outer
        tail, head = outer[:2], outer[2:]
        _, tau1, eta1, tau2, eta2 = merged[v]
        tail2, head2 = split_values(use_2, tau2, eta2, tail, head)
        tail_d, head_d = down(tail2, 2), down(head, 2)
        tail1 = tuple(jnp.where(seg == 2, d, t) for d, t in zip(tail_d, tail))
        head1 = tuple(jnp.where(seg == 2, d, h) for d, h in zip(head_d, head2))
        inner_t, inner_h = split_values(use_1, tau1, eta1, tail1, head1)
        odd = lax.rem(seg, 2) == 1
        for q in range(2):
            tails_in[q].append(jnp.where(odd, down(inner_t, 1)[q], tail1[q]))
            heads_in[q].append(jnp.where(odd, down(head1, 1)[q], inner_h[q]))

    for q in range(2):
        for v in range(5):
            ends_ref[q * 5 + v] = tails_in[q][v]
            ends_ref[10 + q * 5 + v] = heads_in[q][v]

    pl.when(mz < gz - 1)(z_fwd.wait_send)
    pl.when(mz > 0)(z_bwd.wait_send)
    pl.when(me < gy - 1)(y_fwd.wait_send)
    pl.when(me > 0)(y_bwd.wait_send)

    def returns_sent():
        for k in range(1, gy):
            source, target, i = ret(k)
            remote(source, target, yr_s.at[k], yr_r.at[place_of_mine], (i, mz)).wait_send()

    pl.when(owner)(returns_sent) if step > 1 else returns_sent()
    gather_sent(zm_all, zm_s, zm_r)
    gather_sent(zv_all, zv_s, zv_r)


def last_kernel(zval, zspike, ends, out, plane, block, sems):
    copies = []
    for v in range(5):
        t0, t1, h0, h1 = (ends[q * 5 + v] for q in range(4))
        for j in range(ROWS):
            l0, l1, r0, r1 = (zspike[j, q] for q in range(4))
            plane[v, pl.ds(j, 8, stride=STEP), :] = (
                zval[j, v] - (l0 * t0 + l1 * t1) - (r0 * h0 + r1 * h1)
            )
        for g in range(2):
            parts = [plane[v, pl.ds((4 * g + part) * STEP, ROWS), :] for part in range(4)]
            turned = jnp.concatenate(parts, axis=0).T
            block[v, pl.ds(g * HALF, HALF)] = turned.reshape(HALF, 8, 128)
        for x in range(8):
            copies.append(
                pltpu.make_async_copy(
                    block.at[v, :, x], out.at[x, pl.ds(v * ROWS, ROWS)], sems.at[v, x]
                )
            )
            copies[-1].start()
    for copy in copies:
        copy.wait()


def solution(mesh):
    gy, gz = mesh.shape["gy"], mesh.shape["gz"]
    assert gy % 8 == 0
    spec = P(None, None, "gy", "gz")

    def per_device(state, conduct, y_bands, z_bands):
        assert state.shape == (8, 5, ROWS, 128)
        tile = lambda *lead: pltpu.VMEM((*lead, 8, 128), jnp.float32)
        flat = lambda *shape: pltpu.VMEM((*shape, 128), jnp.float32)
        dma = lambda *count: pltpu.SemaphoreType.DMA(count)
        inner = pl.pallas_call(
            functools.partial(kernel, gy, gz),
            out_shape=[tile(ROWS, 5), tile(ROWS, 4), tile(20)],
            in_specs=[pl.BlockSpec(memory_space=pl.ANY)] * 4,
            out_specs=[pl.BlockSpec(memory_space=pltpu.VMEM)] * 3,
            scratch_shapes=[
                tile(5, ROWS), tile(5, ROWS), tile(6, ROWS + 2), tile(2, 2), tile(2, 2),
                tile(ROWS, 5), tile(ROWS, 4), tile(ROWS, 5),
                tile(ROWS, 5),
                flat(5, 8 * STEP), tile(5, ROWS), flat(5, 8 * STEP),
                tile(16), flat(gy, 16), tile(PACK), flat(gy, PACK),
                flat(gy, PACK), tile(PACK),
                tile(gz, 4), tile(gz, 5), tile(gz, 8),
                dma(4, 8), dma(2), dma(2), dma(2), dma(2),
                dma(8), dma(gy), dma(8), dma(gy), dma(gy), dma(8),
                dma(gz), dma(gz), dma(gz), dma(gz), dma(3),
            ],
            compiler_params=pltpu.CompilerParams(collective_id=0, has_side_effects=True),
        )(
            state, conduct, y_bands, z_bands,
        )
        result = pl.pallas_call(
            last_kernel,
            out_shape=jax.ShapeDtypeStruct((8, 5 * ROWS, 128), jnp.float32),
            in_specs=[pl.BlockSpec(memory_space=pltpu.VMEM)] * 3,
            out_specs=pl.BlockSpec(memory_space=pl.ANY),
            scratch_shapes=[flat(5, 8 * STEP), tile(5, ROWS), dma(5, 8)],
        )(*(pltpu.with_memory_space_constraint(x, pltpu.MemorySpace.VMEM) for x in inner))
        return result.reshape(state.shape)

    return jax.shard_map(
        per_device, mesh=mesh, in_specs=(spec, P(None, "gy", "gz"), spec, spec),
        out_specs=spec, check_vma=False,
    )
```

```python
import functools
import jax
import jax.numpy as jnp
from jax import lax
from jax.experimental import pallas as pl
from jax.experimental.pallas import tpu as pltpu
from jax.sharding import PartitionSpec as P

flux_tenth = 0.1
UNROLL = 32
MESH = pl.DeviceIdType.MESH
ROWS = 32
PACK = 20
EDGE = 32
STEP = ROWS + 1
HALF = ROWS // 2


def rows_loop(count, body, carry, unroll=UNROLL):
    if unroll >= count:
        for place in range(count):
            carry = body(place, carry)
        return carry

    def group(number, state):
        for inner in range(unroll):
            state = body(number * unroll + inner, state)
        return state

    return lax.fori_loop(0, count // unroll, group, carry)


def mm(a, b):
    return (
        a[0] * b[0] + a[1] * b[2],
        a[0] * b[1] + a[1] * b[3],
        a[2] * b[0] + a[3] * b[2],
        a[2] * b[1] + a[3] * b[3],
    )


def mv(a, x):
    return (a[0] * x[0] + a[1] * x[1], a[2] * x[0] + a[3] * x[1])


def plus(a, b):
    return tuple(x + y for x, y in zip(a, b))


def minus(a, b):
    return tuple(x - y for x, y in zip(a, b))


def negative(a):
    return tuple(-x for x in a)


def one_minus_inverse(k):
    m00, m01, m10, m11 = 1.0 - k[0], -k[1], -k[2], 1.0 - k[3]
    scale = 1.0 / (m00 * m11 - m01 * m10)
    return (m11 * scale, -m01 * scale, -m10 * scale, m00 * scale)


def factor_segment(band, coefs, spikes, unit=False):
    zero = jnp.zeros((8, 128), jnp.float32)

    def one_row(j, carry, left):
        p1, q1, p2, q2, l01, l11, l02, l12 = carry
        a, b, c, d, e = (band(k, j) for k in range(5))
        red = b - a * p2
        inv = 1.0 / (c - a * q2 - red * p1)
        p = (d - red * q1) * inv
        q = e * inv
        ai = a * inv
        ri = red * inv
        if left == 0:
            l0, l1 = (inv if unit else ai), b * inv
        elif left == 1:
            l0, l1 = -ri * l01, ai - ri * l11
        else:
            l0 = -ai * l02 - ri * l01
            l1 = -ai * l12 - ri * l11
        for number, item in enumerate((ai, ri, inv, p, q)):
            coefs[j, number] = item
        spikes[j, 0] = l0
        spikes[j, 1] = l1
        return (p, q, p1, q1, l0, l1, l01, l11)

    carry = (zero,) * 8
    carry = one_row(0, carry, 0)
    carry = one_row(1, carry, 1)
    carry = rows_loop(ROWS - 2, lambda j, c: one_row(j + 2, c, 2), carry, 30)

    def back(i, carry):
        j = ROWS - 1 - i
        one, two = carry
        p, q = coefs[j, 3], coefs[j, 4]
        last = coefs[j, 2] if unit and i == 0 else zero
        start = (spikes[j, 0], spikes[j, 1], zero, last)
        new = tuple(s - p * x - q * y for s, x, y in zip(start, one, two))
        for number in range(4):
            spikes[j, number] = new[number]
        return (new, one)

    minus_one = zero - 1.0
    beyond = zero if unit else minus_one
    rows_loop(ROWS, back, ((zero, zero, minus_one, zero), (zero, zero, zero, beyond)))


def forward_values(rhs, coefs, values):
    zero = jnp.zeros((8, 128), jnp.float32)

    def row(j, carry):
        one, two = carry
        ai, ri, inv = (coefs[j, k] for k in range(3))
        new = tuple(f * inv - ai * y - ri * x for f, x, y in zip(rhs(j), one, two))
        for number in range(5):
            values[j, number] = new[number]
        return (new, one)

    rows_loop(ROWS, row, ((zero,) * 5, (zero,) * 5))


def backward_values(coefs, values):
    zero = jnp.zeros((8, 128), jnp.float32)

    def row(i, carry):
        j = ROWS - 1 - i
        one, two = carry
        p, q = coefs[j, 3], coefs[j, 4]
        new = tuple(values[j, v] - p * one[v] - q * two[v] for v in range(5))
        for number in range(5):
            values[j, number] = new[number]
        return (new, one)

    rows_loop(ROWS, row, ((zero,) * 5, (zero,) * 5))


def finish_values(values, spikes, tails, heads, put):
    def row(j, carry):
        l0, l1, r0, r1 = (spikes[j, k] for k in range(4))
        for v in range(5):
            put(
                j,
                v,
                values[j, v]
                - (l0 * tails[0][v] + l1 * tails[1][v])
                - (r0 * heads[0][v] + r1 * heads[1][v]),
            )
        return carry

    rows_loop(ROWS, row, 0)


def end_spikes(spikes):
    low, high = (0, 1), (ROWS - 2, ROWS - 1)
    take = lambda rows, first: tuple(spikes[r, first + c] for r in rows for c in range(2))
    return take(low, 0), take(high, 0), take(low, 2), take(high, 2)


def chain_factor(count, matrices):
    factors = []
    beta = None
    for i in range(count):
        lh, lt, rh, rt = matrices(i)
        if i == 0:
            factors.append((None, None, None, None, rh, rt))
            beta = rt
            continue
        m = one_minus_inverse(mm(lh, beta))
        delta = mm(m, rh)
        ltb = mm(lt, beta)
        beta = plus(rt, mm(ltb, delta))
        factors.append((lh, lt, m, ltb, delta, beta))
    return factors


def chain_values(count, factors, ends):
    gammas, alphas = [], []
    for i in range(count):
        gh, gt = ends(i)
        if i:
            lh, lt, m, ltb = factors[i][:4]
            alpha = alphas[-1]
            gh = mv(m, minus(gh, mv(lh, alpha)))
            gt = plus(minus(gt, mv(lt, alpha)), mv(ltb, gh))
        gammas.append(gh)
        alphas.append(gt)
    heads, tails = [None] * count, [None] * count
    heads[-1], tails[-1] = gammas[-1], alphas[-1]
    for i in range(count - 2, -1, -1):
        heads[i] = minus(gammas[i], mv(factors[i][4], heads[i + 1]))
        tails[i] = minus(alphas[i], mv(factors[i][5], heads[i + 1]))
    return heads, tails


def merge_matrices(left, right):
    lha, lta, rha, rta = left
    lhb, ltb, rhb, rtb = right
    n = one_minus_inverse(mm(rta, lhb))
    l_tau = mm(n, lta)
    r_tau = negative(mm(n, mm(rta, rhb)))
    l_eta = negative(mm(lhb, l_tau))
    r_eta = minus(rhb, mm(lhb, r_tau))
    lh = minus(lha, mm(rha, l_eta))
    rh = negative(mm(rha, r_eta))
    lt = negative(mm(ltb, l_tau))
    rt = minus(rtb, mm(ltb, r_tau))
    use = (n, rta, lhb, rha, ltb, l_tau, r_tau, l_eta, r_eta)
    return (lh, lt, rh, rt), use


def merge_values(use, gha, gta, ghb, gtb):
    n, rta, lhb, rha, ltb = use[:5]
    tau = mv(n, minus(gta, mv(rta, ghb)))
    eta = minus(ghb, mv(lhb, tau))
    return minus(gha, mv(rha, eta)), minus(gtb, mv(ltb, tau)), tau, eta


def split_values(use, tau, eta, tail, head):
    l_tau, r_tau, l_eta, r_eta = use[5:]
    inner_tail = minus(minus(tau, mv(l_tau, tail)), mv(r_tau, head))
    inner_head = minus(minus(eta, mv(l_eta, tail)), mv(r_eta, head))
    return inner_tail, inner_head


def up(items, amount):
    return tuple(pltpu.roll(x, 8 - amount, 0) for x in items)


def down(items, amount):
    return tuple(pltpu.roll(x, amount, 0) for x in items)


def flipped(index, mask):
    result, bit = index, 1
    while bit <= mask:
        if mask & bit:
            result = result + bit - 2 * bit * lax.rem(index // bit, 2)
        bit *= 2
    return result


def kernel(
    gy, gz, state_h, conduct_h, yb_h, zb_h, zval, zspike, ends_ref,
    yb, zb, field, zsend, zrecv,
    ycoef, yspike, yval, zcoef, zbt, yplane, plane,
    ym_out, ym_in, yv_out, yv_in, yr_out, yr_in, zm_all, zv_all, ht_all,
    in_sem, zh_s, zh_r, ym_s, ym_r, yv_s, yv_r, yr_s, yr_r,
    zm_s, zm_r, zv_s, zv_r, own_sem,
):
    me, mz = lax.axis_index("gy"), lax.axis_index("gz")
    step = gy // 8
    lanes = lax.broadcasted_iota(jnp.int32, (8, 128), 1)
    subs = lax.broadcasted_iota(jnp.int32, (8, 128), 0)
    seg = lax.rem(subs, 4)
    zero = jnp.zeros((8, 128), jnp.float32)

    loads = [
        [pltpu.make_async_copy(src.at[x], dst(x), in_sem.at[k, x]) for x in range(8)]
        for k, (src, dst) in enumerate(
            (
                (state_h, lambda x: field.at[pl.ds(0, 5), :, x]),
                (conduct_h, lambda x: field.at[5, :, x]),
                (yb_h, lambda x: yb.at[:, :, x]),
                (zb_h, lambda x: zb.at[:, :, x]),
            )
        )
    ]
    for load in loads:
        for copy in load:
            copy.start()

    def loaded(k):
        for copy in loads[k]:
            copy.wait()

    barrier = pltpu.get_barrier_semaphore()
    for k in range(1, gy):
        pl.semaphore_signal(
            barrier, inc=1, device_id=(lax.rem(me + k, gy), mz), device_id_type=MESH
        )
    for k in range(1, gz):
        pl.semaphore_signal(
            barrier, inc=1, device_id=(me, lax.rem(mz + k, gz)), device_id_type=MESH
        )

    loaded(0)
    loaded(1)

    def pack_row(j, carry):
        a0, a1, b0, b1 = carry
        for v in range(6):
            tile = field[v, j]
            place = (v % 4) * ROWS + j
            moved = pltpu.roll(tile, (place + 1) % 128, 1)
            at_a = lanes == place
            at_b = lanes == (place + 1) % 128
            if v < 4:
                a0, b0 = jnp.where(at_a, moved, a0), jnp.where(at_b, moved, b0)
            else:
                a1, b1 = jnp.where(at_a, moved, a1), jnp.where(at_b, moved, b1)
        return (a0, a1, b0, b1)

    a0, a1, b0, b1 = rows_loop(ROWS, pack_row, (zero,) * 4)
    zsend[0, 0], zsend[0, 1], zsend[1, 0], zsend[1, 1] = a0, a1, b0, b1
    pl.semaphore_wait(barrier, gy + gz - 2)

    def remote(src, dst, send, recv, there):
        return pltpu.make_async_remote_copy(
            src_ref=src, dst_ref=dst, send_sem=send, recv_sem=recv,
            device_id=there, device_id_type=MESH,
        )

    prev_z, next_z = lax.rem(mz + gz - 1, gz), lax.rem(mz + 1, gz)
    z_fwd = remote(zsend.at[0], zrecv.at[0], zh_s.at[0], zh_r.at[0], (me, next_z))
    z_bwd = remote(zsend.at[1], zrecv.at[1], zh_s.at[1], zh_r.at[1], (me, prev_z))
    pl.when(mz < gz - 1)(z_fwd.start)
    pl.when(mz > 0)(z_bwd.start)

    @pl.when(mz == 0)
    def _():
        zrecv[0] = jnp.zeros((2, 8, 128), jnp.float32)

    @pl.when(mz == gz - 1)
    def _():
        zrecv[1] = jnp.zeros((2, 8, 128), jnp.float32)

    loaded(2)
    factor_segment(
        lambda k, j: yb[k, j], ycoef, yspike, True
    )
    sent = list(sum(end_spikes(yspike), ())) + [yb[0, 0], yb[4, ROWS - 1]]
    for j in (ROWS - 1, 0):
        sent += [field[v, j] for v in range(6)]
    for number, item in enumerate(sent + [zero, zero]):
        ym_out[number] = item

    place_of_mine = me // step
    owner = lax.rem(me, step) == 0

    def scatter(out, into, send, recv, own, finish):
        for k in (6, 7, 4, 5, 2, 3, 1, 0):
            x = flipped(place_of_mine, k)
            source = out.at[:, x]
            target = into.at[me]
            away = remote(source, target, send.at[k], recv.at[me], (x * step, mz))
            here = pltpu.make_async_copy(source, target, own)
            act = (lambda c: c.wait_send()) if finish else (lambda c: c.start())
            if k:
                act(away)
            else:
                if step > 1:
                    pl.when(jnp.logical_not(owner))(lambda: act(away))
                local = here.wait if finish else here.start
                pl.when(owner)(local) if step > 1 else local()

    def scatter_arrived(out, into, send, recv):
        for k in range(1, gy):
            i = lax.rem(me + k, gy)
            source = out.at[:, 0]
            target = into.at[i]
            remote(source, target, send.at[0], recv.at[i], (i, mz)).wait_recv()

    scatter(ym_out, ym_in, ym_s, ym_r, own_sem.at[0], False)

    first_lane, last_lane = lanes == 0, lanes == 127
    slot = lanes // ROWS

    def own_flux(j, carry):
        k = field[5, j]
        along = jnp.where(last_lane, zero, flux_tenth * (k + pltpu.roll(k, 127, 1)))
        across = flux_tenth * (k + field[5, j + 1]) if j < ROWS - 1 else zero
        new = []
        for v in range(5):
            here = field[v, j]
            z_flow = along * (pltpu.roll(here, 127, 1) - here)
            y_flow = across * (field[v, j + 1] - here) if j < ROWS - 1 else zero
            y_part = y_flow - carry[v] if 0 < j < ROWS - 1 else (y_flow if j == 0 else -carry[v])
            yval[j, v] = here + (y_part + (z_flow - pltpu.roll(z_flow, 1, 1)))
            new.append(y_flow)
        return tuple(new)

    rows_loop(ROWS, own_flux, (zero,) * 5)

    @pl.when(mz > 0)
    def _():
        z_fwd.wait_recv()

    @pl.when(mz < gz - 1)
    def _():
        z_bwd.wait_recv()

    def edge_flux(theirs, ours):
        both = theirs[1] + ours[1]
        k = jnp.where(slot == 0, pltpu.roll(both, 96, 1), both)
        k = jnp.where(slot == 2, pltpu.roll(both, 32, 1), k)
        k = jnp.where(slot == 3, pltpu.roll(both, 64, 1), k)
        return [flux_tenth * k * (x - y) for x, y in zip(theirs, ours)]

    back_one = lambda tiles: [pltpu.roll(t, 127, 1) for t in tiles]
    low = edge_flux([zrecv[0, 0], zrecv[0, 1]], back_one((b0, b1)))
    high = back_one(edge_flux(back_one((zrecv[1, 0], zrecv[1, 1])), (a0, a1)))
    edge = jnp.logical_or(first_lane, last_lane)

    def flux_rhs(j):
        result = []
        for v in range(5):
            place = (v % 4) * ROWS + j
            added = jnp.where(lanes == place, low[v // 4], high[v // 4])
            added = pltpu.roll(added, 128 - place, 1) if place else added
            result.append(yval[j, v] + jnp.where(edge, added, zero))
        return result

    forward_values(flux_rhs, ycoef, yval)
    backward_values(ycoef, yval)
    for number, r in enumerate((0, 1, ROWS - 2, ROWS - 1)):
        for v in range(5):
            yv_out[5 * number + v] = yval[r, v]
    scatter(yv_out, yv_in, yv_s, yv_r, own_sem.at[1], False)

    loaded(3)

    def turn(source, target, k):
        for g in range(2):
            turned = source[k, pl.ds(g * HALF, HALF)].reshape(128, 128).T
            for part in range(4):
                rows = turned[part * ROWS : (part + 1) * ROWS]
                target[k, pl.ds((4 * g + part) * STEP, ROWS), :] = rows

    for k in range(5):
        turn(zb, zbt, k)
    scatter_done = functools.partial(scatter, finish=True)

    def owner_solve():
        scatter_arrived(ym_out, ym_in, ym_s, ym_r)

        wide = lambda i, q: jnp.broadcast_to(ym_in[i, pl.ds(q, 1), :], (8, 128))
        rows = [[wide(i, q) for q in range(18)] for i in range(gy)]

        def matrices(i):
            a, e = rows[i][16:]
            lh, lt = ((g[0] * a, g[1], g[2] * a, g[3]) for g in (rows[i][:4], rows[i][4:8]))
            rh, rt = ((g[0], g[1] * e, g[2], g[3] * e) for g in (rows[i][8:12], rows[i][12:16]))
            return lh, lt, rh, rt

        def edges(i, first):
            if not 0 <= i < gy:
                return zero, zero
            return ym_in[i, pl.ds(first, 8), :], wide(i, first + 5)

        flows = []
        for i in range(gy + 1):
            (s_last, k_last), (s_first, k_first) = edges(i - 1, 18), edges(i, 24)
            flows.append(flux_tenth * (k_last + k_first) * (s_first - s_last))
        factors = chain_factor(gy, matrices)
        added = [
            [rows[i][q + 9] * flows[i + 1] - rows[i][q] * flows[i] for q in (0, 2, 4, 6)]
            for i in range(gy)
        ]
        scatter_arrived(yv_out, yv_in, yv_s, yv_r)

        def ends(i):
            parts = [yv_in[i, pl.ds(5 * q, 5), :] for q in range(4)]
            parts = [jnp.concatenate([x, jnp.zeros((3, 128), jnp.float32)], axis=0) for x in parts]
            parts = plus(parts, added[i])
            return (parts[0], parts[1]), (parts[2], parts[3])

        heads, tails = chain_values(gy, factors, ends)
        for i in range(gy):
            before = tails[i - 1] if i else (zero, zero)
            behind = heads[i + 1] if i < gy - 1 else (zero, zero)
            a, e = rows[i][16:]
            back = (
                a * before[0] + flows[i], before[1],
                behind[0], e * behind[1] - flows[i + 1],
            )
            for q, item in enumerate(back):
                yr_out[i, pl.ds(5 * q, 5), :] = item[0:5]

    def ret(k):
        i = flipped(me, k)
        source = yr_out.at[i]
        target = yr_in.at[:, place_of_mine]
        return source, target, i

    def owner_part():
        scatter_done(ym_out, ym_in, ym_s, ym_r, own_sem.at[0]) if step == 1 else None
        scatter_done(yv_out, yv_in, yv_s, yv_r, own_sem.at[1]) if step == 1 else None
        owner_solve()
        for k in sorted(range(1, gy), key=lambda k: (6, 7, 4, 5, 2, 3, 1).index(k) if k < 8 else -k):
            source, target, i = ret(k)
            remote(source, target, yr_s.at[k], yr_r.at[place_of_mine], (i, mz)).start()
        source, target, i = ret(0)
        pltpu.make_async_copy(source, target, own_sem.at[2]).start()

    if step > 1:
        scatter_done(ym_out, ym_in, ym_s, ym_r, own_sem.at[0])
        scatter_done(yv_out, yv_in, yv_s, yv_r, own_sem.at[1])
        pl.when(owner)(owner_part)
    else:
        owner_part()

    factor_segment(lambda k, j: zbt[k, pl.ds(j, 8, stride=STEP), :], zcoef, zspike)
    level_0 = end_spikes(zspike)
    level_1, use_1 = merge_matrices(level_0, tuple(up(m, 1) for m in level_0))
    level_2, use_2 = merge_matrices(level_1, tuple(up(m, 2) for m in level_1))

    def pack_four(tiles):
        packed = tiles[0]
        for k in range(1, 4):
            packed = jnp.where(seg == k, pltpu.roll(tiles[k], k, 0), packed)
        return packed

    def partners(act):
        for away in range(gz - 1, 0, -1):
            pl.when(mz + away < gz)(functools.partial(act, mz + away))
            pl.when(mz - away >= 0)(functools.partial(act, mz - away))

    def gather(ref, send, recv):
        def act(there):
            remote(ref.at[mz], ref.at[mz], send.at[there], recv.at[mz], (me, there)).start()

        partners(act)

    def gathered(ref, send, recv):
        def act(there):
            remote(ref.at[mz], ref.at[there], send.at[there], recv.at[there], (me, there)).wait_recv()

        partners(act)

    def gather_sent(ref, send, recv):
        def act(there):
            remote(ref.at[mz], ref.at[mz], send.at[there], recv.at[mz], (me, there)).wait_send()

        partners(act)

    for b in range(4):
        zm_all[mz, b] = pack_four(level_2[b])
    gather(zm_all, zm_s, zm_r)

    def y_returned():
        for k in range(8):
            x = flipped(place_of_mine, k)
            target = yr_in.at[:, x]
            away = remote(yr_out.at[0], target, yr_s.at[0], yr_r.at[x], (x * step, mz))
            here = pltpu.make_async_copy(yr_out.at[0], target, own_sem.at[2])
            if k:
                away.wait_recv()
            elif step > 1:
                pl.when(jnp.logical_not(owner))(away.wait_recv)
                pl.when(owner)(here.wait)
            else:
                here.wait()

    y_returned()
    got = [[yr_in[5 * q + v] for v in range(5)] for q in range(4)]

    def put_y(j, v, tile):
        yplane[v, j] = tile

    finish_values(yval, yspike, got[:2], got[2:], put_y)
    for v in range(5):
        turn(yplane, plane, v)

    forward_values(
        lambda j: [plane[v, pl.ds(j, 8, stride=STEP), :] for v in range(5)], zcoef, zval
    )
    backward_values(zcoef, zval)
    merged = []
    for v in range(5):
        gh = (zval[0, v], zval[1, v])
        gt = (zval[ROWS - 2, v], zval[ROWS - 1, v])
        gh1, gt1, tau1, eta1 = merge_values(use_1, gh, gt, up(gh, 1), up(gt, 1))
        gh2, gt2, tau2, eta2 = merge_values(use_2, gh1, gt1, up(gh1, 2), up(gt1, 2))
        merged.append((gh2 + gt2, tau1, eta1, tau2, eta2))
    for q in range(4):
        zv_all[mz, q] = pack_four([merged[v][0][q] for v in range(4)])
    zv_all[mz, 4] = pack_four([merged[4][0][q] for q in range(4)])
    gather(zv_all, zv_s, zv_r)

    gathered(zm_all, zm_s, zm_r)

    def spread(tile, k):
        result = tile
        for r in range(4):
            if r != k:
                result = jnp.where(seg == r, pltpu.roll(tile, (r - k) % 8, 0), result)
        return result

    def z_matrices(i):
        return tuple(tuple(spread(zm_all[i, b], k) for k in range(4)) for b in range(4))

    factors = chain_factor(gz, z_matrices)
    gathered(zv_all, zv_s, zv_r)

    def z_ends(i):
        return (zv_all[i, 0], zv_all[i, 1]), (zv_all[i, 2], zv_all[i, 3])

    def z_ends_last(i):
        tiles = [pltpu.roll(zv_all[i, 4], (8 - q) % 8, 0) if q else zv_all[i, 4] for q in range(4)]
        return (tiles[0], tiles[1]), (tiles[2], tiles[3])

    for number, ends in enumerate((z_ends, z_ends_last)):
        heads, tails = chain_values(gz, factors, ends)
        for i in range(gz):
            before = tails[i - 1] if i else (zero, zero)
            behind = heads[i + 1] if i < gz - 1 else (zero, zero)
            for q, item in enumerate(before + behind):
                ht_all[i, 4 * number + q] = item
    tails_in, heads_in = [[], []], [[], []]
    for v in range(5):
        base, shift = (0, v) if v < 4 else (4, 0)
        outer = tuple(ht_all[mz, base + q] for q in range(4))
        outer = up(outer, shift) if shift else outer
        tail, head = outer[:2], outer[2:]
        _, tau1, eta1, tau2, eta2 = merged[v]
        tail2, head2 = split_values(use_2, tau2, eta2, tail, head)
        tail_d, head_d = down(tail2, 2), down(head, 2)
        tail1 = tuple(jnp.where(seg == 2, d, t) for d, t in zip(tail_d, tail))
        head1 = tuple(jnp.where(seg == 2, d, h) for d, h in zip(head_d, head2))
        inner_t, inner_h = split_values(use_1, tau1, eta1, tail1, head1)
        odd = lax.rem(seg, 2) == 1
        for q in range(2):
            tails_in[q].append(jnp.where(odd, down(inner_t, 1)[q], tail1[q]))
            heads_in[q].append(jnp.where(odd, down(head1, 1)[q], inner_h[q]))

    for q in range(2):
        for v in range(5):
            ends_ref[q * 5 + v] = tails_in[q][v]
            ends_ref[10 + q * 5 + v] = heads_in[q][v]

    pl.when(mz < gz - 1)(z_fwd.wait_send)
    pl.when(mz > 0)(z_bwd.wait_send)

    def returns_sent():
        for k in range(1, gy):
            source, target, i = ret(k)
            remote(source, target, yr_s.at[k], yr_r.at[place_of_mine], (i, mz)).wait_send()

    pl.when(owner)(returns_sent) if step > 1 else returns_sent()
    gather_sent(zm_all, zm_s, zm_r)
    gather_sent(zv_all, zv_s, zv_r)


def last_kernel(zval, zspike, ends, out, plane, block, sems):
    copies = []
    for v in range(5):
        t0, t1, h0, h1 = (ends[q * 5 + v] for q in range(4))
        for j in range(ROWS):
            l0, l1, r0, r1 = (zspike[j, q] for q in range(4))
            plane[v, pl.ds(j, 8, stride=STEP), :] = (
                zval[j, v] - (l0 * t0 + l1 * t1) - (r0 * h0 + r1 * h1)
            )
        for g in range(2):
            parts = [plane[v, pl.ds((4 * g + part) * STEP, ROWS), :] for part in range(4)]
            turned = jnp.concatenate(parts, axis=0).T
            block[v, pl.ds(g * HALF, HALF)] = turned.reshape(HALF, 8, 128)
        for x in range(8):
            copies.append(
                pltpu.make_async_copy(
                    block.at[v, :, x], out.at[x, pl.ds(v * ROWS, ROWS)], sems.at[v, x]
                )
            )
            copies[-1].start()
    for copy in copies:
        copy.wait()


def solution(mesh):
    gy, gz = mesh.shape["gy"], mesh.shape["gz"]
    assert gy % 8 == 0
    spec = P(None, None, "gy", "gz")

    def per_device(state, conduct, y_bands, z_bands):
        assert state.shape == (8, 5, ROWS, 128)
        tile = lambda *lead: pltpu.VMEM((*lead, 8, 128), jnp.float32)
        flat = lambda *shape: pltpu.VMEM((*shape, 128), jnp.float32)
        dma = lambda *count: pltpu.SemaphoreType.DMA(count)
        inner = pl.pallas_call(
            functools.partial(kernel, gy, gz),
            out_shape=[tile(ROWS, 5), tile(ROWS, 4), tile(20)],
            in_specs=[pl.BlockSpec(memory_space=pl.ANY)] * 4,
            out_specs=[pl.BlockSpec(memory_space=pltpu.VMEM)] * 3,
            scratch_shapes=[
                tile(5, ROWS), tile(5, ROWS), tile(6, ROWS), tile(2, 2), tile(2, 2),
                tile(ROWS, 5), tile(ROWS, 4), tile(ROWS, 5),
                tile(ROWS, 5),
                flat(5, 8 * STEP), tile(5, ROWS), flat(5, 8 * STEP),
                tile(EDGE), flat(gy, EDGE), tile(PACK), flat(gy, PACK),
                flat(gy, PACK), tile(PACK),
                tile(gz, 4), tile(gz, 5), tile(gz, 8),
                dma(4, 8), dma(2), dma(2),
                dma(8), dma(gy), dma(8), dma(gy), dma(gy), dma(8),
                dma(gz), dma(gz), dma(gz), dma(gz), dma(3),
            ],
            compiler_params=pltpu.CompilerParams(collective_id=0, has_side_effects=True),
        )(
            state, conduct, y_bands, z_bands,
        )
        result = pl.pallas_call(
            last_kernel,
            out_shape=jax.ShapeDtypeStruct((8, 5 * ROWS, 128), jnp.float32),
            in_specs=[pl.BlockSpec(memory_space=pltpu.VMEM)] * 3,
            out_specs=pl.BlockSpec(memory_space=pl.ANY),
            scratch_shapes=[flat(5, 8 * STEP), tile(5, ROWS), dma(5, 8)],
        )(*(pltpu.with_memory_space_constraint(x, pltpu.MemorySpace.VMEM) for x in inner))
        return result.reshape(state.shape)

    return jax.shard_map(
        per_device, mesh=mesh, in_specs=(spec, P(None, "gy", "gz"), spec, spec),
        out_specs=spec, check_vma=False,
    )
```

```python
import functools
import jax
import jax.numpy as jnp
from jax import lax
from jax.experimental import pallas as pl
from jax.experimental.pallas import tpu as pltpu
from jax.sharding import PartitionSpec as P

flux_tenth = 0.1
UNROLL = 32
MESH = pl.DeviceIdType.MESH
ROWS = 32
PACK = 20
EDGE = 32
STEP = ROWS + 1
HALF = ROWS // 2


def rows_loop(count, body, carry, unroll=UNROLL):
    if unroll >= count:
        for place in range(count):
            carry = body(place, carry)
        return carry

    def group(number, state):
        for inner in range(unroll):
            state = body(number * unroll + inner, state)
        return state

    return lax.fori_loop(0, count // unroll, group, carry)


def mm(a, b):
    return (
        a[0] * b[0] + a[1] * b[2],
        a[0] * b[1] + a[1] * b[3],
        a[2] * b[0] + a[3] * b[2],
        a[2] * b[1] + a[3] * b[3],
    )


def mv(a, x):
    return (a[0] * x[0] + a[1] * x[1], a[2] * x[0] + a[3] * x[1])


def plus(a, b):
    return tuple(x + y for x, y in zip(a, b))


def minus(a, b):
    return tuple(x - y for x, y in zip(a, b))


def negative(a):
    return tuple(-x for x in a)


def one_minus_inverse(k):
    m00, m01, m10, m11 = 1.0 - k[0], -k[1], -k[2], 1.0 - k[3]
    scale = 1.0 / (m00 * m11 - m01 * m10)
    return (m11 * scale, -m01 * scale, -m10 * scale, m00 * scale)


def factor_segment(band, coefs, spikes, unit=False):
    zero = jnp.zeros((8, 128), jnp.float32)

    def one_row(j, carry, left):
        p1, q1, p2, q2, l01, l11, l02, l12 = carry
        a, b, c, d, e = (band(k, j) for k in range(5))
        red = b - a * p2
        inv = 1.0 / (c - a * q2 - red * p1)
        p = (d - red * q1) * inv
        q = e * inv
        ai = a * inv
        ri = red * inv
        if left == 0:
            l0, l1 = (inv if unit else ai), b * inv
        elif left == 1:
            l0, l1 = -ri * l01, ai - ri * l11
        else:
            l0 = -ai * l02 - ri * l01
            l1 = -ai * l12 - ri * l11
        for number, item in enumerate((ai, ri, inv, p, q)):
            coefs[j, number] = item
        spikes[j, 0] = l0
        spikes[j, 1] = l1
        return (p, q, p1, q1, l0, l1, l01, l11)

    carry = (zero,) * 8
    carry = one_row(0, carry, 0)
    carry = one_row(1, carry, 1)
    carry = rows_loop(ROWS - 2, lambda j, c: one_row(j + 2, c, 2), carry, 30)

    def back(i, carry):
        j = ROWS - 1 - i
        one, two = carry
        p, q = coefs[j, 3], coefs[j, 4]
        last = coefs[j, 2] if unit and i == 0 else zero
        start = (spikes[j, 0], spikes[j, 1], zero, last)
        new = tuple(s - p * x - q * y for s, x, y in zip(start, one, two))
        for number in range(4):
            spikes[j, number] = new[number]
        return (new, one)

    minus_one = zero - 1.0
    beyond = zero if unit else minus_one
    rows_loop(ROWS, back, ((zero, zero, minus_one, zero), (zero, zero, zero, beyond)))


def forward_values(rhs, coefs, values):
    zero = jnp.zeros((8, 128), jnp.float32)

    def row(j, carry):
        one, two = carry
        ai, ri, inv = (coefs[j, k] for k in range(3))
        new = tuple(f * inv - ai * y - ri * x for f, x, y in zip(rhs(j), one, two))
        for number in range(5):
            values[j, number] = new[number]
        return (new, one)

    rows_loop(ROWS, row, ((zero,) * 5, (zero,) * 5))


def backward_values(coefs, values):
    zero = jnp.zeros((8, 128), jnp.float32)

    def row(i, carry):
        j = ROWS - 1 - i
        one, two = carry
        p, q = coefs[j, 3], coefs[j, 4]
        new = tuple(values[j, v] - p * one[v] - q * two[v] for v in range(5))
        for number in range(5):
            values[j, number] = new[number]
        return (new, one)

    rows_loop(ROWS, row, ((zero,) * 5, (zero,) * 5))


def finish_values(values, spikes, tails, heads, put):
    def row(j, carry):
        l0, l1, r0, r1 = (spikes[j, k] for k in range(4))
        for v in range(5):
            put(
                j,
                v,
                values[j, v]
                - (l0 * tails[0][v] + l1 * tails[1][v])
                - (r0 * heads[0][v] + r1 * heads[1][v]),
            )
        return carry

    rows_loop(ROWS, row, 0)


def end_spikes(spikes):
    low, high = (0, 1), (ROWS - 2, ROWS - 1)
    take = lambda rows, first: tuple(spikes[r, first + c] for r in rows for c in range(2))
    return take(low, 0), take(high, 0), take(low, 2), take(high, 2)


def chain_factor(count, matrices):
    factors = []
    beta = None
    for i in range(count):
        lh, lt, rh, rt = matrices(i)
        if i == 0:
            factors.append((None, None, None, None, rh, rt))
            beta = rt
            continue
        m = one_minus_inverse(mm(lh, beta))
        delta = mm(m, rh)
        ltb = mm(lt, beta)
        beta = plus(rt, mm(ltb, delta))
        factors.append((lh, lt, m, ltb, delta, beta))
    return factors


def chain_values(count, factors, ends):
    gammas, alphas = [], []
    for i in range(count):
        gh, gt = ends(i)
        if i:
            lh, lt, m, ltb = factors[i][:4]
            alpha = alphas[-1]
            gh = mv(m, minus(gh, mv(lh, alpha)))
            gt = plus(minus(gt, mv(lt, alpha)), mv(ltb, gh))
        gammas.append(gh)
        alphas.append(gt)
    heads, tails = [None] * count, [None] * count
    heads[-1], tails[-1] = gammas[-1], alphas[-1]
    for i in range(count - 2, -1, -1):
        heads[i] = minus(gammas[i], mv(factors[i][4], heads[i + 1]))
        tails[i] = minus(alphas[i], mv(factors[i][5], heads[i + 1]))
    return heads, tails


def merge_matrices(left, right):
    lha, lta, rha, rta = left
    lhb, ltb, rhb, rtb = right
    n = one_minus_inverse(mm(rta, lhb))
    l_tau = mm(n, lta)
    r_tau = negative(mm(n, mm(rta, rhb)))
    l_eta = negative(mm(lhb, l_tau))
    r_eta = minus(rhb, mm(lhb, r_tau))
    lh = minus(lha, mm(rha, l_eta))
    rh = negative(mm(rha, r_eta))
    lt = negative(mm(ltb, l_tau))
    rt = minus(rtb, mm(ltb, r_tau))
    use = (n, rta, lhb, rha, ltb, l_tau, r_tau, l_eta, r_eta)
    return (lh, lt, rh, rt), use


def merge_values(use, gha, gta, ghb, gtb):
    n, rta, lhb, rha, ltb = use[:5]
    tau = mv(n, minus(gta, mv(rta, ghb)))
    eta = minus(ghb, mv(lhb, tau))
    return minus(gha, mv(rha, eta)), minus(gtb, mv(ltb, tau)), tau, eta


def split_values(use, tau, eta, tail, head):
    l_tau, r_tau, l_eta, r_eta = use[5:]
    inner_tail = minus(minus(tau, mv(l_tau, tail)), mv(r_tau, head))
    inner_head = minus(minus(eta, mv(l_eta, tail)), mv(r_eta, head))
    return inner_tail, inner_head


def up(items, amount):
    return tuple(pltpu.roll(x, 8 - amount, 0) for x in items)


def down(items, amount):
    return tuple(pltpu.roll(x, amount, 0) for x in items)


def flipped(index, mask):
    result, bit = index, 1
    while bit <= mask:
        if mask & bit:
            result = result + bit - 2 * bit * lax.rem(index // bit, 2)
        bit *= 2
    return result


def kernel(
    gy, gz, state_h, conduct_h, yb_h, zb_h, zval, zspike, ends_ref,
    yb, zb, field, zsend, zrecv,
    ycoef, yspike, yval, zcoef, zbt, yplane, plane,
    ym_out, ym_in, yv_out, yv_in, yr_out, yr_in, zm_all, zv_all, ht_all,
    in_sem, zh_s, zh_r, ym_s, ym_r, yv_s, yv_r, yr_s, yr_r,
    zm_s, zm_r, zv_s, zv_r, own_sem,
):
    me, mz = lax.axis_index("gy"), lax.axis_index("gz")
    step = gy // 8
    lanes = lax.broadcasted_iota(jnp.int32, (8, 128), 1)
    subs = lax.broadcasted_iota(jnp.int32, (8, 128), 0)
    seg = lax.rem(subs, 4)
    zero = jnp.zeros((8, 128), jnp.float32)

    loads = [
        [pltpu.make_async_copy(src.at[x], dst(x), in_sem.at[k, x]) for x in range(8)]
        for k, (src, dst) in enumerate(
            (
                (state_h, lambda x: field.at[pl.ds(0, 5), :, x]),
                (conduct_h, lambda x: field.at[5, :, x]),
                (yb_h, lambda x: yb.at[:, :, x]),
                (zb_h, lambda x: zb.at[:, :, x]),
            )
        )
    ]
    for load in loads:
        for copy in load:
            copy.start()

    def loaded(k):
        for copy in loads[k]:
            copy.wait()

    barrier = pltpu.get_barrier_semaphore()
    for k in range(1, gy):
        pl.semaphore_signal(
            barrier, inc=1, device_id=(lax.rem(me + k, gy), mz), device_id_type=MESH
        )
    for k in range(1, gz):
        pl.semaphore_signal(
            barrier, inc=1, device_id=(me, lax.rem(mz + k, gz)), device_id_type=MESH
        )

    loaded(0)
    loaded(1)

    def pack_row(j, carry):
        a0, a1, b0, b1 = carry
        for v in range(6):
            tile = field[v, j]
            place = (v % 4) * ROWS + j
            moved = pltpu.roll(tile, (place + 1) % 128, 1)
            at_a = lanes == place
            at_b = lanes == (place + 1) % 128
            if v < 4:
                a0, b0 = jnp.where(at_a, moved, a0), jnp.where(at_b, moved, b0)
            else:
                a1, b1 = jnp.where(at_a, moved, a1), jnp.where(at_b, moved, b1)
        return (a0, a1, b0, b1)

    a0, a1, b0, b1 = rows_loop(ROWS, pack_row, (zero,) * 4)
    zsend[0, 0], zsend[0, 1], zsend[1, 0], zsend[1, 1] = a0, a1, b0, b1
    pl.semaphore_wait(barrier, gy + gz - 2)

    def remote(src, dst, send, recv, there):
        return pltpu.make_async_remote_copy(
            src_ref=src, dst_ref=dst, send_sem=send, recv_sem=recv,
            device_id=there, device_id_type=MESH,
        )

    prev_z, next_z = lax.rem(mz + gz - 1, gz), lax.rem(mz + 1, gz)
    z_fwd = remote(zsend.at[0], zrecv.at[0], zh_s.at[0], zh_r.at[0], (me, next_z))
    z_bwd = remote(zsend.at[1], zrecv.at[1], zh_s.at[1], zh_r.at[1], (me, prev_z))
    pl.when(mz < gz - 1)(z_fwd.start)
    pl.when(mz > 0)(z_bwd.start)

    @pl.when(mz == 0)
    def _():
        zrecv[0] = jnp.zeros((2, 8, 128), jnp.float32)

    @pl.when(mz == gz - 1)
    def _():
        zrecv[1] = jnp.zeros((2, 8, 128), jnp.float32)

    loaded(2)
    factor_segment(
        lambda k, j: yb[k, j], ycoef, yspike, True
    )
    sent = list(sum(end_spikes(yspike), ())) + [yb[0, 0], yb[4, ROWS - 1]]
    for j in (ROWS - 1, 0):
        sent += [field[v, j] for v in range(6)]
    for number, item in enumerate(sent + [zero, zero]):
        ym_out[number] = item

    place_of_mine = me // step
    owner = lax.rem(me, step) == 0

    def scatter(out, into, send, recv, own, finish):
        for k in (6, 7, 4, 5, 2, 3, 1, 0):
            x = flipped(place_of_mine, k)
            source = out.at[:, x]
            target = into.at[me]
            away = remote(source, target, send.at[k], recv.at[me], (x * step, mz))
            here = pltpu.make_async_copy(source, target, own)
            act = (lambda c: c.wait_send()) if finish else (lambda c: c.start())
            if k:
                act(away)
            else:
                if step > 1:
                    pl.when(jnp.logical_not(owner))(lambda: act(away))
                if not finish:
                    pl.when(owner)(here.start) if step > 1 else here.start()

    def scatter_own(out, into, own):
        pltpu.make_async_copy(out.at[:, 0], into.at[me], own).wait()

    def scatter_arrived(out, into, send, recv):
        for k in range(1, gy):
            i = lax.rem(me + k, gy)
            source = out.at[:, 0]
            target = into.at[i]
            remote(source, target, send.at[0], recv.at[i], (i, mz)).wait_recv()

    scatter(ym_out, ym_in, ym_s, ym_r, own_sem.at[0], False)

    first_lane, last_lane = lanes == 0, lanes == 127
    slot = lanes // ROWS

    def own_flux(j, carry):
        k = field[5, j]
        upward = jnp.where(last_lane, zero, flux_tenth * (k + pltpu.roll(k, 127, 1)))
        downward = jnp.where(first_lane, zero, flux_tenth * (k + pltpu.roll(k, 1, 1)))
        across = flux_tenth * (k + field[5, j + 1]) if j < ROWS - 1 else zero
        new = []
        for v in range(5):
            here = field[v, j]
            before, after = pltpu.roll(here, 1, 1), pltpu.roll(here, 127, 1)
            y_flow = across * (field[v, j + 1] - here) if j < ROWS - 1 else zero
            y_part = y_flow - carry[v] if 0 < j < ROWS - 1 else (y_flow if j == 0 else -carry[v])
            z_part = upward * (after - here) - downward * (here - before)
            yval[j, v] = here + (y_part + z_part)
            new.append(y_flow)
        return tuple(new)

    rows_loop(ROWS, own_flux, (zero,) * 5)

    @pl.when(mz > 0)
    def _():
        z_fwd.wait_recv()

    @pl.when(mz < gz - 1)
    def _():
        z_bwd.wait_recv()

    def edge_flux(theirs, ours):
        both = theirs[1] + ours[1]
        k = jnp.where(slot == 0, pltpu.roll(both, 96, 1), both)
        k = jnp.where(slot == 2, pltpu.roll(both, 32, 1), k)
        k = jnp.where(slot == 3, pltpu.roll(both, 64, 1), k)
        return [flux_tenth * k * (x - y) for x, y in zip(theirs, ours)]

    back_one = lambda tiles: [pltpu.roll(t, 127, 1) for t in tiles]
    low = edge_flux([zrecv[0, 0], zrecv[0, 1]], back_one((b0, b1)))
    high = back_one(edge_flux(back_one((zrecv[1, 0], zrecv[1, 1])), (a0, a1)))
    edge = jnp.logical_or(first_lane, last_lane)

    def flux_rhs(j):
        result = []
        for v in range(5):
            place = (v % 4) * ROWS + j
            added = jnp.where(lanes == place, low[v // 4], high[v // 4])
            added = pltpu.roll(added, 128 - place, 1) if place else added
            result.append(yval[j, v] + jnp.where(edge, added, zero))
        return result

    forward_values(flux_rhs, ycoef, yval)
    backward_values(ycoef, yval)
    for number, r in enumerate((0, 1, ROWS - 2, ROWS - 1)):
        for v in range(5):
            yv_out[5 * number + v] = yval[r, v]
    scatter(yv_out, yv_in, yv_s, yv_r, own_sem.at[1], False)

    loaded(3)

    def turn(source, target, k):
        for g in range(2):
            turned = source[k, pl.ds(g * HALF, HALF)].reshape(128, 128).T
            for part in range(4):
                rows = turned[part * ROWS : (part + 1) * ROWS]
                target[k, pl.ds((4 * g + part) * STEP, ROWS), :] = rows

    for k in range(5):
        turn(zb, zbt, k)
    scatter_done = functools.partial(scatter, finish=True)

    def owner_solve():
        scatter_arrived(ym_out, ym_in, ym_s, ym_r)

        wide = lambda i, q: jnp.broadcast_to(ym_in[i, pl.ds(q, 1), :], (8, 128))
        rows = [[wide(i, q) for q in range(18)] for i in range(gy)]

        def matrices(i):
            a, e = rows[i][16:]
            lh, lt = ((g[0] * a, g[1], g[2] * a, g[3]) for g in (rows[i][:4], rows[i][4:8]))
            rh, rt = ((g[0], g[1] * e, g[2], g[3] * e) for g in (rows[i][8:12], rows[i][12:16]))
            return lh, lt, rh, rt

        def edges(i, first):
            if not 0 <= i < gy:
                return zero, zero
            return ym_in[i, pl.ds(first, 8), :], wide(i, first + 5)

        flows = []
        for i in range(gy + 1):
            (s_last, k_last), (s_first, k_first) = edges(i - 1, 18), edges(i, 24)
            flows.append(flux_tenth * (k_last + k_first) * (s_first - s_last))
        factors = chain_factor(gy, matrices)
        added = [
            [rows[i][q + 9] * flows[i + 1] - rows[i][q] * flows[i] for q in (0, 2, 4, 6)]
            for i in range(gy)
        ]
        scatter_arrived(yv_out, yv_in, yv_s, yv_r)

        def ends(i):
            parts = [yv_in[i, pl.ds(5 * q, 5), :] for q in range(4)]
            parts = [jnp.concatenate([x, jnp.zeros((3, 128), jnp.float32)], axis=0) for x in parts]
            parts = plus(parts, added[i])
            return (parts[0], parts[1]), (parts[2], parts[3])

        heads, tails = chain_values(gy, factors, ends)
        for i in range(gy):
            before = tails[i - 1] if i else (zero, zero)
            behind = heads[i + 1] if i < gy - 1 else (zero, zero)
            a, e = rows[i][16:]
            back = (
                a * before[0] + flows[i], before[1],
                behind[0], e * behind[1] - flows[i + 1],
            )
            for q, item in enumerate(back):
                yr_out[i, pl.ds(5 * q, 5), :] = item[0:5]

    def ret(k):
        i = flipped(me, k)
        source = yr_out.at[i]
        target = yr_in.at[:, place_of_mine]
        return source, target, i

    def owner_part():
        scatter_own(ym_out, ym_in, own_sem.at[0])
        scatter_own(yv_out, yv_in, own_sem.at[1])
        owner_solve()
        for k in sorted(range(1, gy), key=lambda k: (6, 7, 4, 5, 2, 3, 1).index(k) if k < 8 else -k):
            source, target, i = ret(k)
            remote(source, target, yr_s.at[k], yr_r.at[place_of_mine], (i, mz)).start()
        source, target, i = ret(0)
        pltpu.make_async_copy(source, target, own_sem.at[2]).start()

    factor_segment(lambda k, j: zbt[k, pl.ds(j, 8, stride=STEP), :], zcoef, zspike)
    level_0 = end_spikes(zspike)
    level_1, use_1 = merge_matrices(level_0, tuple(up(m, 1) for m in level_0))
    level_2, use_2 = merge_matrices(level_1, tuple(up(m, 2) for m in level_1))

    def pack_four(tiles):
        packed = tiles[0]
        for k in range(1, 4):
            packed = jnp.where(seg == k, pltpu.roll(tiles[k], k, 0), packed)
        return packed

    def partners(act):
        for away in range(gz - 1, 0, -1):
            pl.when(mz + away < gz)(functools.partial(act, mz + away))
            pl.when(mz - away >= 0)(functools.partial(act, mz - away))

    def gather(ref, send, recv):
        def act(there):
            remote(ref.at[mz], ref.at[mz], send.at[there], recv.at[mz], (me, there)).start()

        partners(act)

    def gathered(ref, send, recv):
        def act(there):
            remote(ref.at[mz], ref.at[there], send.at[there], recv.at[there], (me, there)).wait_recv()

        partners(act)

    def gather_sent(ref, send, recv):
        def act(there):
            remote(ref.at[mz], ref.at[mz], send.at[there], recv.at[mz], (me, there)).wait_send()

        partners(act)

    for b in range(4):
        zm_all[mz, b] = pack_four(level_2[b])
    gather(zm_all, zm_s, zm_r)

    pl.when(owner)(owner_part) if step > 1 else owner_part()

    def y_returned():
        for k in range(8):
            x = flipped(place_of_mine, k)
            target = yr_in.at[:, x]
            away = remote(yr_out.at[0], target, yr_s.at[0], yr_r.at[x], (x * step, mz))
            here = pltpu.make_async_copy(yr_out.at[0], target, own_sem.at[2])
            if k:
                away.wait_recv()
            elif step > 1:
                pl.when(jnp.logical_not(owner))(away.wait_recv)
                pl.when(owner)(here.wait)
            else:
                here.wait()

    y_returned()
    got = [[yr_in[5 * q + v] for v in range(5)] for q in range(4)]

    def put_y(j, v, tile):
        yplane[v, j] = tile

    finish_values(yval, yspike, got[:2], got[2:], put_y)
    for v in range(5):
        turn(yplane, plane, v)

    forward_values(
        lambda j: [plane[v, pl.ds(j, 8, stride=STEP), :] for v in range(5)], zcoef, zval
    )
    backward_values(zcoef, zval)
    merged = []
    for v in range(5):
        gh = (zval[0, v], zval[1, v])
        gt = (zval[ROWS - 2, v], zval[ROWS - 1, v])
        gh1, gt1, tau1, eta1 = merge_values(use_1, gh, gt, up(gh, 1), up(gt, 1))
        gh2, gt2, tau2, eta2 = merge_values(use_2, gh1, gt1, up(gh1, 2), up(gt1, 2))
        merged.append((gh2 + gt2, tau1, eta1, tau2, eta2))
    for q in range(4):
        zv_all[mz, q] = pack_four([merged[v][0][q] for v in range(4)])
    zv_all[mz, 4] = pack_four([merged[4][0][q] for q in range(4)])
    gather(zv_all, zv_s, zv_r)

    gathered(zm_all, zm_s, zm_r)

    def spread(tile, k):
        result = tile
        for r in range(4):
            if r != k:
                result = jnp.where(seg == r, pltpu.roll(tile, (r - k) % 8, 0), result)
        return result

    def z_matrices(i):
        return tuple(tuple(spread(zm_all[i, b], k) for k in range(4)) for b in range(4))

    factors = chain_factor(gz, z_matrices)
    gathered(zv_all, zv_s, zv_r)

    def z_ends(i):
        return (zv_all[i, 0], zv_all[i, 1]), (zv_all[i, 2], zv_all[i, 3])

    def z_ends_last(i):
        tiles = [pltpu.roll(zv_all[i, 4], (8 - q) % 8, 0) if q else zv_all[i, 4] for q in range(4)]
        return (tiles[0], tiles[1]), (tiles[2], tiles[3])

    for number, ends in enumerate((z_ends, z_ends_last)):
        heads, tails = chain_values(gz, factors, ends)
        for i in range(gz):
            before = tails[i - 1] if i else (zero, zero)
            behind = heads[i + 1] if i < gz - 1 else (zero, zero)
            for q, item in enumerate(before + behind):
                ht_all[i, 4 * number + q] = item
    tails_in, heads_in = [[], []], [[], []]
    for v in range(5):
        base, shift = (0, v) if v < 4 else (4, 0)
        outer = tuple(ht_all[mz, base + q] for q in range(4))
        outer = up(outer, shift) if shift else outer
        tail, head = outer[:2], outer[2:]
        _, tau1, eta1, tau2, eta2 = merged[v]
        tail2, head2 = split_values(use_2, tau2, eta2, tail, head)
        tail_d, head_d = down(tail2, 2), down(head, 2)
        tail1 = tuple(jnp.where(seg == 2, d, t) for d, t in zip(tail_d, tail))
        head1 = tuple(jnp.where(seg == 2, d, h) for d, h in zip(head_d, head2))
        inner_t, inner_h = split_values(use_1, tau1, eta1, tail1, head1)
        odd = lax.rem(seg, 2) == 1
        for q in range(2):
            tails_in[q].append(jnp.where(odd, down(inner_t, 1)[q], tail1[q]))
            heads_in[q].append(jnp.where(odd, down(head1, 1)[q], inner_h[q]))

    for q in range(2):
        for v in range(5):
            ends_ref[q * 5 + v] = tails_in[q][v]
            ends_ref[10 + q * 5 + v] = heads_in[q][v]

    pl.when(mz < gz - 1)(z_fwd.wait_send)
    pl.when(mz > 0)(z_bwd.wait_send)

    def returns_sent():
        for k in range(1, gy):
            source, target, i = ret(k)
            remote(source, target, yr_s.at[k], yr_r.at[place_of_mine], (i, mz)).wait_send()

    pl.when(owner)(returns_sent) if step > 1 else returns_sent()
    scatter_done(ym_out, ym_in, ym_s, ym_r, own_sem.at[0])
    scatter_done(yv_out, yv_in, yv_s, yv_r, own_sem.at[1])
    gather_sent(zm_all, zm_s, zm_r)
    gather_sent(zv_all, zv_s, zv_r)


def last_kernel(zval, zspike, ends, out, plane, block, sems):
    copies = []
    for v in range(5):
        t0, t1, h0, h1 = (ends[q * 5 + v] for q in range(4))
        for j in range(ROWS):
            l0, l1, r0, r1 = (zspike[j, q] for q in range(4))
            plane[v, pl.ds(j, 8, stride=STEP), :] = (
                zval[j, v] - (l0 * t0 + l1 * t1) - (r0 * h0 + r1 * h1)
            )
        for g in range(2):
            parts = [plane[v, pl.ds((4 * g + part) * STEP, ROWS), :] for part in range(4)]
            turned = jnp.concatenate(parts, axis=0).T
            block[v, pl.ds(g * HALF, HALF)] = turned.reshape(HALF, 8, 128)
        for x in range(8):
            copies.append(
                pltpu.make_async_copy(
                    block.at[v, :, x], out.at[x, pl.ds(v * ROWS, ROWS)], sems.at[v, x]
                )
            )
            copies[-1].start()
    for copy in copies:
        copy.wait()


def solution(mesh):
    gy, gz = mesh.shape["gy"], mesh.shape["gz"]
    assert gy % 8 == 0
    spec = P(None, None, "gy", "gz")

    def per_device(state, conduct, y_bands, z_bands):
        assert state.shape == (8, 5, ROWS, 128)
        tile = lambda *lead: pltpu.VMEM((*lead, 8, 128), jnp.float32)
        flat = lambda *shape: pltpu.VMEM((*shape, 128), jnp.float32)
        dma = lambda *count: pltpu.SemaphoreType.DMA(count)
        inner = pl.pallas_call(
            functools.partial(kernel, gy, gz),
            out_shape=[tile(ROWS, 5), tile(ROWS, 4), tile(20)],
            in_specs=[pl.BlockSpec(memory_space=pl.ANY)] * 4,
            out_specs=[pl.BlockSpec(memory_space=pltpu.VMEM)] * 3,
            scratch_shapes=[
                tile(5, ROWS), tile(5, ROWS), tile(6, ROWS), tile(2, 2), tile(2, 2),
                tile(ROWS, 5), tile(ROWS, 4), tile(ROWS, 5),
                tile(ROWS, 5),
                flat(5, 8 * STEP), tile(5, ROWS), flat(5, 8 * STEP),
                tile(EDGE), flat(gy, EDGE), tile(PACK), flat(gy, PACK),
                flat(gy, PACK), tile(PACK),
                tile(gz, 4), tile(gz, 5), tile(gz, 8),
                dma(4, 8), dma(2), dma(2),
                dma(8), dma(gy), dma(8), dma(gy), dma(gy), dma(8),
                dma(gz), dma(gz), dma(gz), dma(gz), dma(3),
            ],
            compiler_params=pltpu.CompilerParams(collective_id=0, has_side_effects=True),
        )(
            state, conduct, y_bands, z_bands,
        )
        result = pl.pallas_call(
            last_kernel,
            out_shape=jax.ShapeDtypeStruct((8, 5 * ROWS, 128), jnp.float32),
            in_specs=[pl.BlockSpec(memory_space=pltpu.VMEM)] * 3,
            out_specs=pl.BlockSpec(memory_space=pl.ANY),
            scratch_shapes=[flat(5, 8 * STEP), tile(5, ROWS), dma(5, 8)],
        )(*(pltpu.with_memory_space_constraint(x, pltpu.MemorySpace.VMEM) for x in inner))
        return result.reshape(state.shape)

    return jax.shard_map(
        per_device, mesh=mesh, in_specs=(spec, P(None, "gy", "gz"), spec, spec),
        out_specs=spec, check_vma=False,
    )
```

```python
import functools
import jax
import jax.numpy as jnp
from jax import lax
from jax.experimental import pallas as pl
from jax.experimental.pallas import tpu as pltpu
from jax.sharding import PartitionSpec as P

flux_tenth = 0.1
UNROLL = 32
MESH = pl.DeviceIdType.MESH
ROWS = 32
PACK = 20
EDGE = 32
STEP = ROWS + 1
HALF = ROWS // 2


def rows_loop(count, body, carry, unroll=UNROLL):
    if unroll >= count:
        for place in range(count):
            carry = body(place, carry)
        return carry

    def group(number, state):
        for inner in range(unroll):
            state = body(number * unroll + inner, state)
        return state

    return lax.fori_loop(0, count // unroll, group, carry)


def mm(a, b):
    return (
        a[0] * b[0] + a[1] * b[2],
        a[0] * b[1] + a[1] * b[3],
        a[2] * b[0] + a[3] * b[2],
        a[2] * b[1] + a[3] * b[3],
    )


def mv(a, x):
    return (a[0] * x[0] + a[1] * x[1], a[2] * x[0] + a[3] * x[1])


def plus(a, b):
    return tuple(x + y for x, y in zip(a, b))


def minus(a, b):
    return tuple(x - y for x, y in zip(a, b))


def negative(a):
    return tuple(-x for x in a)


def one_minus_inverse(k):
    m00, m01, m10, m11 = 1.0 - k[0], -k[1], -k[2], 1.0 - k[3]
    scale = 1.0 / (m00 * m11 - m01 * m10)
    return (m11 * scale, -m01 * scale, -m10 * scale, m00 * scale)


def factor_segment(band, coefs, spikes, unit=False):
    zero = jnp.zeros((8, 128), jnp.float32)

    def one_row(j, carry, left):
        p1, q1, p2, q2, l01, l11, l02, l12 = carry
        a, b, c, d, e = (band(k, j) for k in range(5))
        red = b - a * p2
        inv = 1.0 / (c - a * q2 - red * p1)
        p = (d - red * q1) * inv
        q = e * inv
        ai = a * inv
        ri = red * inv
        if left == 0:
            l0, l1 = (inv if unit else ai), b * inv
        elif left == 1:
            l0, l1 = -ri * l01, ai - ri * l11
        else:
            l0 = -ai * l02 - ri * l01
            l1 = -ai * l12 - ri * l11
        for number, item in enumerate((ai, ri, inv, p, q)):
            coefs[j, number] = item
        spikes[j, 0] = l0
        spikes[j, 1] = l1
        return (p, q, p1, q1, l0, l1, l01, l11)

    carry = (zero,) * 8
    carry = one_row(0, carry, 0)
    carry = one_row(1, carry, 1)
    carry = rows_loop(ROWS - 2, lambda j, c: one_row(j + 2, c, 2), carry, 30)

    def back(i, carry):
        j = ROWS - 1 - i
        one, two = carry
        p, q = coefs[j, 3], coefs[j, 4]
        last = coefs[j, 2] if unit and i == 0 else zero
        start = (spikes[j, 0], spikes[j, 1], zero, last)
        new = tuple(s - p * x - q * y for s, x, y in zip(start, one, two))
        for number in range(4):
            spikes[j, number] = new[number]
        return (new, one)

    minus_one = zero - 1.0
    beyond = zero if unit else minus_one
    rows_loop(ROWS, back, ((zero, zero, minus_one, zero), (zero, zero, zero, beyond)))


def forward_values(rhs, coefs, values):
    zero = jnp.zeros((8, 128), jnp.float32)

    def row(j, carry):
        one, two = carry
        ai, ri, inv = (coefs[j, k] for k in range(3))
        new = tuple(f * inv - ai * y - ri * x for f, x, y in zip(rhs(j), one, two))
        for number in range(5):
            values[j, number] = new[number]
        return (new, one)

    rows_loop(ROWS, row, ((zero,) * 5, (zero,) * 5))


def backward_values(coefs, values):
    zero = jnp.zeros((8, 128), jnp.float32)

    def row(i, carry):
        j = ROWS - 1 - i
        one, two = carry
        p, q = coefs[j, 3], coefs[j, 4]
        new = tuple(values[j, v] - p * one[v] - q * two[v] for v in range(5))
        for number in range(5):
            values[j, number] = new[number]
        return (new, one)

    rows_loop(ROWS, row, ((zero,) * 5, (zero,) * 5))


def finish_values(values, spikes, tails, heads, put):
    def row(j, carry):
        l0, l1, r0, r1 = (spikes[j, k] for k in range(4))
        for v in range(5):
            put(
                j,
                v,
                values[j, v]
                - (l0 * tails[0][v] + l1 * tails[1][v])
                - (r0 * heads[0][v] + r1 * heads[1][v]),
            )
        return carry

    rows_loop(ROWS, row, 0)


def end_spikes(spikes):
    low, high = (0, 1), (ROWS - 2, ROWS - 1)
    take = lambda rows, first: tuple(spikes[r, first + c] for r in rows for c in range(2))
    return take(low, 0), take(high, 0), take(low, 2), take(high, 2)


def chain_factor(count, matrices):
    factors = []
    beta = None
    for i in range(count):
        lh, lt, rh, rt = matrices(i)
        if i == 0:
            factors.append((None, None, None, None, rh, rt))
            beta = rt
            continue
        m = one_minus_inverse(mm(lh, beta))
        delta = mm(m, rh)
        ltb = mm(lt, beta)
        beta = plus(rt, mm(ltb, delta))
        factors.append((lh, lt, m, ltb, delta, beta))
    return factors


def chain_values(count, factors, ends):
    gammas, alphas = [], []
    for i in range(count):
        gh, gt = ends(i)
        if i:
            lh, lt, m, ltb = factors[i][:4]
            alpha = alphas[-1]
            gh = mv(m, minus(gh, mv(lh, alpha)))
            gt = plus(minus(gt, mv(lt, alpha)), mv(ltb, gh))
        gammas.append(gh)
        alphas.append(gt)
    heads, tails = [None] * count, [None] * count
    heads[-1], tails[-1] = gammas[-1], alphas[-1]
    for i in range(count - 2, -1, -1):
        heads[i] = minus(gammas[i], mv(factors[i][4], heads[i + 1]))
        tails[i] = minus(alphas[i], mv(factors[i][5], heads[i + 1]))
    return heads, tails


def merge_matrices(left, right):
    lha, lta, rha, rta = left
    lhb, ltb, rhb, rtb = right
    n = one_minus_inverse(mm(rta, lhb))
    l_tau = mm(n, lta)
    r_tau = negative(mm(n, mm(rta, rhb)))
    l_eta = negative(mm(lhb, l_tau))
    r_eta = minus(rhb, mm(lhb, r_tau))
    lh = minus(lha, mm(rha, l_eta))
    rh = negative(mm(rha, r_eta))
    lt = negative(mm(ltb, l_tau))
    rt = minus(rtb, mm(ltb, r_tau))
    use = (n, rta, lhb, rha, ltb, l_tau, r_tau, l_eta, r_eta)
    return (lh, lt, rh, rt), use


def merge_values(use, gha, gta, ghb, gtb):
    n, rta, lhb, rha, ltb = use[:5]
    tau = mv(n, minus(gta, mv(rta, ghb)))
    eta = minus(ghb, mv(lhb, tau))
    return minus(gha, mv(rha, eta)), minus(gtb, mv(ltb, tau)), tau, eta


def split_values(use, tau, eta, tail, head):
    l_tau, r_tau, l_eta, r_eta = use[5:]
    inner_tail = minus(minus(tau, mv(l_tau, tail)), mv(r_tau, head))
    inner_head = minus(minus(eta, mv(l_eta, tail)), mv(r_eta, head))
    return inner_tail, inner_head


def up(items, amount):
    return tuple(pltpu.roll(x, 8 - amount, 0) for x in items)


def down(items, amount):
    return tuple(pltpu.roll(x, amount, 0) for x in items)


def flipped(index, mask):
    result, bit = index, 1
    while bit <= mask:
        if mask & bit:
            result = result + bit - 2 * bit * lax.rem(index // bit, 2)
        bit *= 2
    return result


def kernel(
    gy, gz, state_h, conduct_h, yb_h, zb_h, zval, zspike, ends_ref,
    yb, zb, field, zsend, zrecv,
    ycoef, yspike, yval, zcoef, zbt, yplane, plane,
    ym_out, ym_in, yv_out, yv_in, yr_out, yr_in, zm_all, zv_all, ht_all,
    in_sem, zh_s, zh_r, ym_s, ym_r, yv_s, yv_r, yr_s, yr_r,
    zm_s, zm_r, zv_s, zv_r, own_sem,
):
    me, mz = lax.axis_index("gy"), lax.axis_index("gz")
    step = gy // 8
    lanes = lax.broadcasted_iota(jnp.int32, (8, 128), 1)
    subs = lax.broadcasted_iota(jnp.int32, (8, 128), 0)
    seg = lax.rem(subs, 4)
    zero = jnp.zeros((8, 128), jnp.float32)

    loads = [
        [pltpu.make_async_copy(src.at[x], dst(x), in_sem.at[k, x]) for x in range(8)]
        for k, (src, dst) in enumerate(
            (
                (state_h, lambda x: field.at[pl.ds(0, 5), :, x]),
                (conduct_h, lambda x: field.at[5, :, x]),
                (yb_h, lambda x: yb.at[:, :, x]),
                (zb_h, lambda x: zb.at[:, :, x]),
            )
        )
    ]
    def start_loads(*numbers):
        for k in numbers:
            for copy in loads[k]:
                copy.start()

    start_loads(0, 1)

    def loaded(k):
        for copy in loads[k]:
            copy.wait()

    barrier = pltpu.get_barrier_semaphore()
    for k in range(1, gy):
        pl.semaphore_signal(
            barrier, inc=1, device_id=(lax.rem(me + k, gy), mz), device_id_type=MESH
        )
    for k in range(1, gz):
        pl.semaphore_signal(
            barrier, inc=1, device_id=(me, lax.rem(mz + k, gz)), device_id_type=MESH
        )

    loaded(0)
    loaded(1)
    start_loads(2, 3)

    def pack_row(j, carry):
        a0, a1, b0, b1 = carry
        for v in range(6):
            tile = field[v, j]
            place = (v % 4) * ROWS + j
            moved = pltpu.roll(tile, (place + 1) % 128, 1)
            at_a = lanes == place
            at_b = lanes == (place + 1) % 128
            if v < 4:
                a0, b0 = jnp.where(at_a, moved, a0), jnp.where(at_b, moved, b0)
            else:
                a1, b1 = jnp.where(at_a, moved, a1), jnp.where(at_b, moved, b1)
        return (a0, a1, b0, b1)

    a0, a1, b0, b1 = rows_loop(ROWS, pack_row, (zero,) * 4)
    zsend[0, 0], zsend[0, 1], zsend[1, 0], zsend[1, 1] = a0, a1, b0, b1
    pl.semaphore_wait(barrier, gy + gz - 2)

    def remote(src, dst, send, recv, there):
        return pltpu.make_async_remote_copy(
            src_ref=src, dst_ref=dst, send_sem=send, recv_sem=recv,
            device_id=there, device_id_type=MESH,
        )

    prev_z, next_z = lax.rem(mz + gz - 1, gz), lax.rem(mz + 1, gz)
    z_fwd = remote(zsend.at[0], zrecv.at[0], zh_s.at[0], zh_r.at[0], (me, next_z))
    z_bwd = remote(zsend.at[1], zrecv.at[1], zh_s.at[1], zh_r.at[1], (me, prev_z))
    pl.when(mz < gz - 1)(z_fwd.start)
    pl.when(mz > 0)(z_bwd.start)

    @pl.when(mz == 0)
    def _():
        zrecv[0] = jnp.zeros((2, 8, 128), jnp.float32)

    @pl.when(mz == gz - 1)
    def _():
        zrecv[1] = jnp.zeros((2, 8, 128), jnp.float32)

    loaded(2)
    factor_segment(
        lambda k, j: yb[k, j], ycoef, yspike, True
    )
    sent = list(sum(end_spikes(yspike), ())) + [yb[0, 0], yb[4, ROWS - 1]]
    for j in (ROWS - 1, 0):
        sent += [field[v, j] for v in range(6)]
    for number, item in enumerate(sent + [zero, zero]):
        ym_out[number] = item

    place_of_mine = me // step
    owner = lax.rem(me, step) == 0

    def scatter(out, into, send, recv, own, finish):
        for k in (6, 7, 4, 5, 2, 3, 1, 0):
            x = flipped(place_of_mine, k)
            source = out.at[:, x]
            target = into.at[me]
            away = remote(source, target, send.at[k], recv.at[me], (x * step, mz))
            here = pltpu.make_async_copy(source, target, own)
            act = (lambda c: c.wait_send()) if finish else (lambda c: c.start())
            if k:
                act(away)
            else:
                if step > 1:
                    pl.when(jnp.logical_not(owner))(lambda: act(away))
                if not finish:
                    pl.when(owner)(here.start) if step > 1 else here.start()

    def scatter_own(out, into, own):
        pltpu.make_async_copy(out.at[:, 0], into.at[me], own).wait()

    def scatter_arrived(out, into, send, recv):
        for k in range(1, gy):
            i = lax.rem(me + k, gy)
            source = out.at[:, 0]
            target = into.at[i]
            remote(source, target, send.at[0], recv.at[i], (i, mz)).wait_recv()

    scatter(ym_out, ym_in, ym_s, ym_r, own_sem.at[0], False)

    first_lane, last_lane = lanes == 0, lanes == 127
    slot = lanes // ROWS

    def own_flux(j, carry):
        k = field[5, j]
        upward = jnp.where(last_lane, zero, flux_tenth * (k + pltpu.roll(k, 127, 1)))
        downward = jnp.where(first_lane, zero, flux_tenth * (k + pltpu.roll(k, 1, 1)))
        across = flux_tenth * (k + field[5, j + 1]) if j < ROWS - 1 else zero
        new = []
        for v in range(5):
            here = field[v, j]
            before, after = pltpu.roll(here, 1, 1), pltpu.roll(here, 127, 1)
            y_flow = across * (field[v, j + 1] - here) if j < ROWS - 1 else zero
            y_part = y_flow - carry[v] if 0 < j < ROWS - 1 else (y_flow if j == 0 else -carry[v])
            z_part = upward * (after - here) - downward * (here - before)
            yval[j, v] = here + (y_part + z_part)
            new.append(y_flow)
        return tuple(new)

    rows_loop(ROWS, own_flux, (zero,) * 5)

    @pl.when(mz > 0)
    def _():
        z_fwd.wait_recv()

    @pl.when(mz < gz - 1)
    def _():
        z_bwd.wait_recv()

    def edge_flux(theirs, ours):
        both = theirs[1] + ours[1]
        k = jnp.where(slot == 0, pltpu.roll(both, 96, 1), both)
        k = jnp.where(slot == 2, pltpu.roll(both, 32, 1), k)
        k = jnp.where(slot == 3, pltpu.roll(both, 64, 1), k)
        return [flux_tenth * k * (x - y) for x, y in zip(theirs, ours)]

    back_one = lambda tiles: [pltpu.roll(t, 127, 1) for t in tiles]
    low = edge_flux([zrecv[0, 0], zrecv[0, 1]], back_one((b0, b1)))
    high = back_one(edge_flux(back_one((zrecv[1, 0], zrecv[1, 1])), (a0, a1)))
    edge = jnp.logical_or(first_lane, last_lane)

    def flux_rhs(j):
        result = []
        for v in range(5):
            place = (v % 4) * ROWS + j
            added = jnp.where(lanes == place, low[v // 4], high[v // 4])
            added = pltpu.roll(added, 128 - place, 1) if place else added
            result.append(yval[j, v] + jnp.where(edge, added, zero))
        return result

    forward_values(flux_rhs, ycoef, yval)
    backward_values(ycoef, yval)
    for number, r in enumerate((0, 1, ROWS - 2, ROWS - 1)):
        for v in range(5):
            yv_out[5 * number + v] = yval[r, v]
    scatter(yv_out, yv_in, yv_s, yv_r, own_sem.at[1], False)

    loaded(3)

    def turn(source, target, k):
        for g in range(2):
            turned = source[k, pl.ds(g * HALF, HALF)].reshape(128, 128).T
            for part in range(4):
                rows = turned[part * ROWS : (part + 1) * ROWS]
                target[k, pl.ds((4 * g + part) * STEP, ROWS), :] = rows

    for k in range(5):
        turn(zb, zbt, k)
    scatter_done = functools.partial(scatter, finish=True)

    def owner_solve():
        scatter_arrived(ym_out, ym_in, ym_s, ym_r)

        wide = lambda i, q: jnp.broadcast_to(ym_in[i, pl.ds(q, 1), :], (8, 128))
        rows = [[wide(i, q) for q in range(18)] for i in range(gy)]

        def matrices(i):
            a, e = rows[i][16:]
            lh, lt = ((g[0] * a, g[1], g[2] * a, g[3]) for g in (rows[i][:4], rows[i][4:8]))
            rh, rt = ((g[0], g[1] * e, g[2], g[3] * e) for g in (rows[i][8:12], rows[i][12:16]))
            return lh, lt, rh, rt

        def edges(i, first):
            if not 0 <= i < gy:
                return zero, zero
            return ym_in[i, pl.ds(first, 8), :], wide(i, first + 5)

        flows = []
        for i in range(gy + 1):
            (s_last, k_last), (s_first, k_first) = edges(i - 1, 18), edges(i, 24)
            flows.append(flux_tenth * (k_last + k_first) * (s_first - s_last))
        factors = chain_factor(gy, matrices)
        added = [
            [rows[i][q + 9] * flows[i + 1] - rows[i][q] * flows[i] for q in (0, 2, 4, 6)]
            for i in range(gy)
        ]
        scatter_arrived(yv_out, yv_in, yv_s, yv_r)

        def ends(i):
            parts = [yv_in[i, pl.ds(5 * q, 5), :] for q in range(4)]
            parts = [jnp.concatenate([x, jnp.zeros((3, 128), jnp.float32)], axis=0) for x in parts]
            parts = plus(parts, added[i])
            return (parts[0], parts[1]), (parts[2], parts[3])

        heads, tails = chain_values(gy, factors, ends)
        for i in range(gy):
            before = tails[i - 1] if i else (zero, zero)
            behind = heads[i + 1] if i < gy - 1 else (zero, zero)
            a, e = rows[i][16:]
            back = (
                a * before[0] + flows[i], before[1],
                behind[0], e * behind[1] - flows[i + 1],
            )
            for q, item in enumerate(back):
                yr_out[i, pl.ds(5 * q, 5), :] = item[0:5]

    def ret(k):
        i = flipped(me, k)
        source = yr_out.at[i]
        target = yr_in.at[:, place_of_mine]
        return source, target, i

    def owner_part():
        scatter_own(ym_out, ym_in, own_sem.at[0])
        scatter_own(yv_out, yv_in, own_sem.at[1])
        owner_solve()
        for k in sorted(range(1, gy), key=lambda k: (6, 7, 4, 5, 2, 3, 1).index(k) if k < 8 else -k):
            source, target, i = ret(k)
            remote(source, target, yr_s.at[k], yr_r.at[place_of_mine], (i, mz)).start()
        source, target, i = ret(0)
        pltpu.make_async_copy(source, target, own_sem.at[2]).start()

    factor_segment(lambda k, j: zbt[k, pl.ds(j, 8, stride=STEP), :], zcoef, zspike)
    level_0 = end_spikes(zspike)
    level_1, use_1 = merge_matrices(level_0, tuple(up(m, 1) for m in level_0))
    level_2, use_2 = merge_matrices(level_1, tuple(up(m, 2) for m in level_1))

    def pack_four(tiles):
        packed = tiles[0]
        for k in range(1, 4):
            packed = jnp.where(seg == k, pltpu.roll(tiles[k], k, 0), packed)
        return packed

    def partners(act):
        for away in range(gz - 1, 0, -1):
            pl.when(mz + away < gz)(functools.partial(act, mz + away))
            pl.when(mz - away >= 0)(functools.partial(act, mz - away))

    def gather(ref, send, recv):
        def act(there):
            remote(ref.at[mz], ref.at[mz], send.at[there], recv.at[mz], (me, there)).start()

        partners(act)

    def gathered(ref, send, recv):
        def act(there):
            remote(ref.at[mz], ref.at[there], send.at[there], recv.at[there], (me, there)).wait_recv()

        partners(act)

    def gather_sent(ref, send, recv):
        def act(there):
            remote(ref.at[mz], ref.at[mz], send.at[there], recv.at[mz], (me, there)).wait_send()

        partners(act)

    def parts_of(device):
        ends = (device == 0, device == gz - 1)
        middle = jnp.logical_not(jnp.logical_or(*ends))
        return zip((*ends, middle), (pl.ds(2, 3), pl.ds(0, 3), pl.ds(0, 5)))

    def values_out(finish):
        def act(there):
            for wanted, part in parts_of(mz):
                mine = zv_all.at[mz, part]
                away = remote(mine, mine, zv_s.at[there], zv_r.at[mz], (me, there))
                pl.when(wanted)(away.wait_send if finish else away.start)

        partners(act)

    def values_in():
        def act(there):
            for wanted, part in parts_of(there):
                theirs = zv_all.at[there, part]
                away = remote(
                    zv_all.at[mz, part], theirs, zv_s.at[there], zv_r.at[there], (me, there)
                )
                pl.when(wanted)(away.wait_recv)

        partners(act)

    for b in range(4):
        zm_all[mz, b] = pack_four(level_2[b])
    gather(zm_all, zm_s, zm_r)

    pl.when(owner)(owner_part) if step > 1 else owner_part()

    def y_returned():
        for k in range(8):
            x = flipped(place_of_mine, k)
            target = yr_in.at[:, x]
            away = remote(yr_out.at[0], target, yr_s.at[0], yr_r.at[x], (x * step, mz))
            here = pltpu.make_async_copy(yr_out.at[0], target, own_sem.at[2])
            if k:
                away.wait_recv()
            elif step > 1:
                pl.when(jnp.logical_not(owner))(away.wait_recv)
                pl.when(owner)(here.wait)
            else:
                here.wait()

    y_returned()
    got = [[yr_in[5 * q + v] for v in range(5)] for q in range(4)]

    def put_y(j, v, tile):
        yplane[v, j] = tile

    finish_values(yval, yspike, got[:2], got[2:], put_y)
    for v in range(5):
        turn(yplane, plane, v)

    forward_values(
        lambda j: [plane[v, pl.ds(j, 8, stride=STEP), :] for v in range(5)], zcoef, zval
    )
    backward_values(zcoef, zval)
    merged = []
    for v in range(5):
        gh = (zval[0, v], zval[1, v])
        gt = (zval[ROWS - 2, v], zval[ROWS - 1, v])
        gh1, gt1, tau1, eta1 = merge_values(use_1, gh, gt, up(gh, 1), up(gt, 1))
        gh2, gt2, tau2, eta2 = merge_values(use_2, gh1, gt1, up(gh1, 2), up(gt1, 2))
        merged.append((gh2 + gt2, tau1, eta1, tau2, eta2))
    for q in range(4):
        zv_all[mz, (0, 1, 3, 4)[q]] = pack_four([merged[v][0][q] for v in range(4)])
    zv_all[mz, 2] = pack_four([merged[4][0][q] for q in range(4)])
    values_out(False)

    gathered(zm_all, zm_s, zm_r)

    def spread(tile, k):
        result = tile
        for r in range(4):
            if r != k:
                result = jnp.where(seg == r, pltpu.roll(tile, (r - k) % 8, 0), result)
        return result

    def z_matrices(i):
        return tuple(tuple(spread(zm_all[i, b], k) for k in range(4)) for b in range(4))

    factors = chain_factor(gz, z_matrices)
    values_in()

    def z_ends(i):
        return (zv_all[i, 0], zv_all[i, 1]), (zv_all[i, 3], zv_all[i, 4])

    def z_ends_last(i):
        tiles = [pltpu.roll(zv_all[i, 2], (8 - q) % 8, 0) if q else zv_all[i, 2] for q in range(4)]
        return (tiles[0], tiles[1]), (tiles[2], tiles[3])

    for number, ends in enumerate((z_ends, z_ends_last)):
        heads, tails = chain_values(gz, factors, ends)
        for i in range(gz):
            before = tails[i - 1] if i else (zero, zero)
            behind = heads[i + 1] if i < gz - 1 else (zero, zero)
            for q, item in enumerate(before + behind):
                ht_all[i, 4 * number + q] = item
    tails_in, heads_in = [[], []], [[], []]
    for v in range(5):
        base, shift = (0, v) if v < 4 else (4, 0)
        outer = tuple(ht_all[mz, base + q] for q in range(4))
        outer = up(outer, shift) if shift else outer
        tail, head = outer[:2], outer[2:]
        _, tau1, eta1, tau2, eta2 = merged[v]
        tail2, head2 = split_values(use_2, tau2, eta2, tail, head)
        tail_d, head_d = down(tail2, 2), down(head, 2)
        tail1 = tuple(jnp.where(seg == 2, d, t) for d, t in zip(tail_d, tail))
        head1 = tuple(jnp.where(seg == 2, d, h) for d, h in zip(head_d, head2))
        inner_t, inner_h = split_values(use_1, tau1, eta1, tail1, head1)
        odd = lax.rem(seg, 2) == 1
        for q in range(2):
            tails_in[q].append(jnp.where(odd, down(inner_t, 1)[q], tail1[q]))
            heads_in[q].append(jnp.where(odd, down(head1, 1)[q], inner_h[q]))

    for q in range(2):
        for v in range(5):
            ends_ref[q * 5 + v] = tails_in[q][v]
            ends_ref[10 + q * 5 + v] = heads_in[q][v]

    pl.when(mz < gz - 1)(z_fwd.wait_send)
    pl.when(mz > 0)(z_bwd.wait_send)

    def returns_sent():
        for k in range(1, gy):
            source, target, i = ret(k)
            remote(source, target, yr_s.at[k], yr_r.at[place_of_mine], (i, mz)).wait_send()

    pl.when(owner)(returns_sent) if step > 1 else returns_sent()
    scatter_done(ym_out, ym_in, ym_s, ym_r, own_sem.at[0])
    scatter_done(yv_out, yv_in, yv_s, yv_r, own_sem.at[1])
    gather_sent(zm_all, zm_s, zm_r)
    values_out(True)


def last_kernel(zval, zspike, ends, out, plane, block, sems):
    copies = []
    for v in range(5):
        t0, t1, h0, h1 = (ends[q * 5 + v] for q in range(4))
        for j in range(ROWS):
            l0, l1, r0, r1 = (zspike[j, q] for q in range(4))
            plane[v, pl.ds(j, 8, stride=STEP), :] = (
                zval[j, v] - (l0 * t0 + l1 * t1) - (r0 * h0 + r1 * h1)
            )
        for g in range(2):
            parts = [plane[v, pl.ds((4 * g + part) * STEP, ROWS), :] for part in range(4)]
            turned = jnp.concatenate(parts, axis=0).T
            block[v, pl.ds(g * HALF, HALF)] = turned.reshape(HALF, 8, 128)
        for x in range(8):
            copies.append(
                pltpu.make_async_copy(
                    block.at[v, :, x], out.at[x, pl.ds(v * ROWS, ROWS)], sems.at[v, x]
                )
            )
            copies[-1].start()
    for copy in copies:
        copy.wait()


def solution(mesh):
    gy, gz = mesh.shape["gy"], mesh.shape["gz"]
    assert gy % 8 == 0
    spec = P(None, None, "gy", "gz")

    def per_device(state, conduct, y_bands, z_bands):
        assert state.shape == (8, 5, ROWS, 128)
        tile = lambda *lead: pltpu.VMEM((*lead, 8, 128), jnp.float32)
        flat = lambda *shape: pltpu.VMEM((*shape, 128), jnp.float32)
        dma = lambda *count: pltpu.SemaphoreType.DMA(count)
        inner = pl.pallas_call(
            functools.partial(kernel, gy, gz),
            out_shape=[tile(ROWS, 5), tile(ROWS, 4), tile(20)],
            in_specs=[pl.BlockSpec(memory_space=pl.ANY)] * 4,
            out_specs=[pl.BlockSpec(memory_space=pltpu.VMEM)] * 3,
            scratch_shapes=[
                tile(5, ROWS), tile(5, ROWS), tile(6, ROWS), tile(2, 2), tile(2, 2),
                tile(ROWS, 5), tile(ROWS, 4), tile(ROWS, 5),
                tile(ROWS, 5),
                flat(5, 8 * STEP), tile(5, ROWS), flat(5, 8 * STEP),
                tile(EDGE), flat(gy, EDGE), tile(PACK), flat(gy, PACK),
                flat(gy, PACK), tile(PACK),
                tile(gz, 4), tile(gz, 5), tile(gz, 8),
                dma(4, 8), dma(2), dma(2),
                dma(8), dma(gy), dma(8), dma(gy), dma(gy), dma(8),
                dma(gz), dma(gz), dma(gz), dma(gz), dma(3),
            ],
            compiler_params=pltpu.CompilerParams(collective_id=0, has_side_effects=True),
        )(
            state, conduct, y_bands, z_bands,
        )
        result = pl.pallas_call(
            last_kernel,
            out_shape=jax.ShapeDtypeStruct((8, 5 * ROWS, 128), jnp.float32),
            in_specs=[pl.BlockSpec(memory_space=pltpu.VMEM)] * 3,
            out_specs=pl.BlockSpec(memory_space=pl.ANY),
            scratch_shapes=[flat(5, 8 * STEP), tile(5, ROWS), dma(5, 8)],
        )(*(pltpu.with_memory_space_constraint(x, pltpu.MemorySpace.VMEM) for x in inner))
        return result.reshape(state.shape)

    return jax.shard_map(
        per_device, mesh=mesh, in_specs=(spec, P(None, "gy", "gz"), spec, spec),
        out_specs=spec, check_vma=False,
    )
```
